32 devices in a mesh: wide: 8 (over z, core), narrow: 4 (over y, x).
Axes of the slice: x: 2, y: 2, z: 4, core: 2. Of those that a mesh axis runs over, the one named last changes fastest.
Arguments:
- tokens: bfloat16 [4, 8, 4, 256, 768], P('narrow', 'wide'), may hold values from -6 to 6
- segment_ids: int32 [4, 8, 4, 256], P('narrow', 'wide'), may hold values from -1 to 7, as said below
- cotangent: bfloat16 [4, 8, 4, 256, 768], P('narrow', 'wide'), may hold values from -6 to 6
- w_qkv: bfloat16 [768, 2304], replicated, may hold values from -0.21875 to 0.21875
- b_qv: float32 [1536], replicated, may hold values from -3 to 3
- w_out: bfloat16 [768, 768], replicated, may hold values from -0.875 to 0.875
- b_out: float32 [768], replicated, may hold values from -3 to 3
- ls_attn: float32 [768], replicated, may hold values from 0.25 to 1.75
- ln1_gain: float32 [768], replicated, may hold values from 0.25 to 1.75
- ln1_bias: float32 [768], replicated, may hold values from -3 to 3
- ln2_gain: float32 [768], replicated, may hold values from 0.25 to 1.75
- ln2_bias: float32 [768], replicated, may hold values from -3 to 3
- w_fc1: bfloat16 [768, 3072], replicated, may hold values from -0.21875 to 0.21875
- b_fc1: float32 [3072], replicated, may hold values from -3 to 3
- w_fc2: bfloat16 [3072, 768], replicated, may hold values from -0.109375 to 0.109375
- b_fc2: float32 [768], replicated, may hold values from -3 to 3
- ls_mlp: float32 [768], replicated, may hold values from 0.25 to 1.75
Outputs:
- output: bfloat16 [4, 8, 4, 256, 768], P('narrow', 'wide')
- grad_tokens: bfloat16 [4, 8, 4, 256, 768], P('narrow', 'wide')
- grad_w_qkv: float32 [768, 2304], P('narrow')
- grad_b_qv: float32 [1536], P('narrow')
- grad_w_out: float32 [768, 768], P('narrow')
- grad_b_out: float32 [768], P('narrow')
- grad_ls_attn: float32 [768], P('narrow')
- grad_ln1_gain: float32 [768], P('narrow')
- grad_ln1_bias: float32 [768], P('narrow')
- grad_ln2_gain: float32 [768], P('narrow')
- grad_ln2_bias: float32 [768], P('narrow')
- grad_w_fc1: float32 [768, 3072], P('narrow')
- grad_b_fc1: float32 [3072], P('narrow')
- grad_w_fc2: float32 [3072, 768], P('narrow')
- grad_b_fc2: float32 [768], P('narrow')
- grad_ls_mlp: float32 [768], P('narrow')
The draws below stay inside these ranges and needn't reach their ends.
Inputs may be any that keep to these rules, and one draw needn't show every extreme that they name: `segment_ids`: in each block, images take consecutive slots from the block's first slot on; the slots of one image share an id of 0 to 7 and different images of a block have different ids; -1 marks the padding after the last image. An image holds k * k + 5 slots for a whole k, at most 1374 and at most 2048; the first image of block 0 is the longest such image.
All inputs are finite; a program needn't handle non-finite values.
Results may differ from the reference program's by a relative error of at most 0.018.
Values may be sent and summed in bfloat16 or wider, within the bound.
A program may use at most 256 MiB of HBM per device.

```python
import math
import jax
import jax.numpy as jnp
from jax import lax

D = 768
HEADS = 12
HEAD = 64
FF = 3072
GROUPS = 4
BLOCK = 2048
ROWS = 4
SPANS = 8
PIECE = 256
BLOCKS = 16


def draw_segment_ids(key, part):
    blocks = ROWS * GROUPS
    largest = min(37, math.isqrt(BLOCK - 5))
    smallest = min(7, max(2, largest // 2))
    grid_sides = jax.random.randint(key, (blocks, 8), smallest, largest + 1)
    grid_sides = grid_sides.at[0, 0].set(largest)
    lengths = grid_sides * grid_sides + 5
    filled = jnp.zeros((blocks,), jnp.int32)
    places = jnp.arange(BLOCK, dtype=jnp.int32)[None, :]
    labels = jnp.full((blocks, BLOCK), -1, jnp.int32)
    for number in range(8):
        length = lengths[:, number]
        fitting = filled + length <= BLOCK
        inside = fitting[:, None] & (places >= filled[:, None]) & (places < (filled + length)[:, None])
        labels = jnp.where(inside, number, labels)
        filled = jnp.where(fitting, filled + length, filled)
    return labels.reshape(ROWS, GROUPS, SPANS, PIECE).transpose(0, 2, 1, 3)


def level_of(stream_key, extent, cuts, least, high):
    level, own = 1.0, jax.random.fold_in(stream_key, 6)
    for dim, parts in cuts:
        draws = jnp.exp(jax.random.uniform(jax.random.fold_in(own, dim), (parts,), jnp.float32, least / len(cuts), high / len(cuts)))
        level = level * jnp.repeat(draws, extent[dim] // parts).reshape([-1 if axis == dim else 1 for axis in range(len(extent))])
    return level


def noise(rng, shape, spread, bound, shards=(), kind=jnp.bfloat16):
    level = level_of(rng, shape, shards, -0.22, 0.18) if shards else 1.0
    entries = jax.random.normal(rng, shape, jnp.float32) * spread * level
    return jnp.minimum(jnp.maximum(entries, -bound), bound).astype(kind)


def setup_inputs(seed: int = 0) -> dict:
    streams_of = jax.random.split(jax.random.key(seed), 18)
    return {
        "tokens": noise(streams_of[0], (ROWS, SPANS, GROUPS, PIECE, D), 1.0, 6.0, ((0, 4), (1, 8))),
        "segment_ids": draw_segment_ids(jax.random.fold_in(streams_of[17], 71), 0),
        "cotangent": noise(streams_of[2], (ROWS, SPANS, GROUPS, PIECE, D), 1.0, 6.0, ((0, 4), (1, 8))),
        "w_qkv": noise(streams_of[3], (D, 3 * D), D ** -0.5, 0.21875),
        "b_qv": noise(streams_of[4], (2 * D,), 0.5, 3.0, (), jnp.float32),
        "w_out": noise(streams_of[5], (D, D), (D // 16) ** -0.5, 0.875),
        "b_out": noise(streams_of[6], (D,), 0.5, 3.0, (), jnp.float32),
        "ls_attn": jnp.clip(1.0 + 0.15 * jax.random.normal(streams_of[7], (D,), jnp.float32), 0.25, 1.75),
        "ln1_gain": jnp.clip(1.0 + 0.15 * jax.random.normal(streams_of[8], (D,), jnp.float32), 0.25, 1.75),
        "ln1_bias": noise(streams_of[9], (D,), 0.5, 3.0, (), jnp.float32),
        "ln2_gain": jnp.clip(1.0 + 0.15 * jax.random.normal(streams_of[10], (D,), jnp.float32), 0.25, 1.75),
        "ln2_bias": noise(streams_of[11], (D,), 0.5, 3.0, (), jnp.float32),
        "w_fc1": noise(streams_of[12], (D, FF), D ** -0.5, 0.21875),
        "b_fc1": noise(streams_of[13], (FF,), 0.5, 3.0, (), jnp.float32),
        "w_fc2": noise(streams_of[14], (FF, D), FF ** -0.5, 0.109375),
        "b_fc2": noise(streams_of[15], (D,), 0.5, 3.0, (), jnp.float32),
        "ls_mlp": jnp.clip(1.0 + 0.15 * jax.random.normal(streams_of[16], (D,), jnp.float32), 0.25, 1.75),
    }


EPSILON = 1e-06
ROOT_HALF = 0.7071067811865476
HIGH = lax.Precision.HIGHEST

@jax.custom_vjp
def low(v):
    return lax.optimization_barrier(v.astype(jnp.bfloat16)).astype(jnp.float32)

@jax.custom_vjp
def low_back(v):
    return v

def low_keep(v):
    return (low(v), None)

def low_pass(kept, grad):
    return (grad,)

def back_keep(v):
    return (v, None)

def back_low(kept, grad):
    return (low(grad),)
low.defvjp(low_keep, low_pass)
low_back.defvjp(back_keep, back_low)

def layer_norm(values, gain, bias):
    average = lax.optimization_barrier(jnp.mean(values, -1, keepdims=True))
    centred = values - average
    variance = lax.optimization_barrier(jnp.mean(centred * centred, -1, keepdims=True))
    return centred * lax.rsqrt(variance + EPSILON) * gain + bias

def gelu_exact(values):
    return 0.5 * values * (1.0 + lax.erf(values * ROOT_HALF))

def layer_block(weights, block_tokens, block_ids):
    w_qkv, b_qv, w_out, b_out, ls_attn, ln1_gain, ln1_bias, ln2_gain, ln2_bias, w_fc1, b_fc1, w_fc2, b_fc2, ls_mlp = weights
    valid_rows = (block_ids >= 0).astype(jnp.float32)[:, None]
    normed = low(layer_norm(block_tokens, ln1_gain, ln1_bias))
    bias_all = jnp.concatenate([b_qv[:D], jnp.zeros((D,), jnp.float32), b_qv[D:]])
    qkv = low_back(low(jnp.dot(normed, w_qkv, precision=HIGH) + bias_all))
    triples = qkv.reshape(BLOCK, 3, HEADS, HEAD)
    raw_scores = jnp.einsum('qhd,khd->hqk', triples[:, 0], triples[:, 1], precision=HIGH) * HEAD ** (-0.5)
    scores = low_back(raw_scores)
    same_image = block_ids[:, None] == block_ids[None, :]
    scores = jnp.where(same_image[None], scores, -1e+30)
    row_max = lax.optimization_barrier(jnp.max(scores, -1, keepdims=True))
    shifted = jnp.exp(scores - row_max)
    soft = shifted / lax.optimization_barrier(jnp.sum(shifted, -1, keepdims=True))
    mixed = jnp.einsum('hqk,khd->qhd', low(soft), triples[:, 2], precision=HIGH)
    mixed = low_back(low(mixed.reshape(BLOCK, D)))
    projected = low_back(jnp.dot(mixed, w_out, precision=HIGH) + b_out)
    hidden = block_tokens + ls_attn * projected
    second = low(layer_norm(hidden, ln2_gain, ln2_bias))
    pre_act = low_back(jnp.dot(second, w_fc1, precision=HIGH) + b_fc1)
    activation = low(gelu_exact(pre_act))
    mlp_out = low_back(jnp.dot(activation, w_fc2, precision=HIGH) + b_fc2)
    return (hidden + ls_mlp * mlp_out) * valid_rows

def reference(tokens, segment_ids, cotangent, w_qkv, b_qv, w_out, b_out, ls_attn, ln1_gain, ln1_bias, ln2_gain, ln2_bias, w_fc1, b_fc1, w_fc2, b_fc2, ls_mlp):

    def to_blocks(array_in):
        return array_in.astype(jnp.float32).transpose(0, 2, 1, 3, 4).reshape(BLOCKS, BLOCK, D)

    def from_blocks(array_in):
        return array_in.reshape(ROWS, GROUPS, SPANS, PIECE, D).transpose(0, 2, 1, 3, 4).astype(jnp.bfloat16)
    block_ids = segment_ids.transpose(0, 2, 1, 3).reshape(BLOCKS, BLOCK)
    weights = tuple((member.astype(jnp.float32) for member in (w_qkv, b_qv, w_out, b_out, ls_attn, ln1_gain, ln1_bias, ln2_gain, ln2_bias, w_fc1, b_fc1, w_fc2, b_fc2, ls_mlp)))

    def forward(block_inputs, params):
        single = jax.checkpoint(lambda pair: layer_block(params, pair[0], pair[1]))
        return lax.map(single, (block_inputs, block_ids))
    result, pullback = jax.vjp(forward, to_blocks(tokens), weights)
    grad_inputs, grads = pullback(to_blocks(cotangent))
    return (from_blocks(result), from_blocks(grad_inputs), grads[0], grads[1], grads[2], grads[3], grads[4], grads[5], grads[6], grads[7], grads[8], grads[9], grads[10], grads[11], grads[12], grads[13])
```

```python
import functools
import jax
import jax.numpy as jnp
from jax import lax
from jax.experimental import pallas as pl
from jax.experimental.pallas import tpu as pltpu
from jax.sharding import PartitionSpec as P

D = 768
HEADS = 12
HEAD = 64
GROUPS = 4
TILE = 256
LANES = 128
EPSILON = 1e-06
ROOT_HALF = 0.7071067811865476
FAR = -1e30
F32 = jnp.float32
BF16 = jnp.bfloat16


def layer_norm(values, gain, bias):
    average = jnp.mean(values, -1, keepdims=True)
    centred = values - average
    variance = jnp.mean(centred * centred, -1, keepdims=True)
    return centred * lax.rsqrt(variance + EPSILON) * gain + bias


def gelu_exact(values):
    return 0.5 * values * (1.0 + lax.erf(values * ROOT_HALF))


def dot_nt(a, b):
    return lax.dot_general(a, b, (((1,), (1,)), ((), ())), preferred_element_type=F32)


def dot_nn(a, b):
    return jnp.dot(a, b, preferred_element_type=F32)


class Geometry:
    def __init__(self, wide, piece):
        self.wide = wide
        self.piece = piece
        self.peers = wide // GROUPS
        self.chunk = piece // self.peers
        self.rows = wide * self.chunk
        self.slots = wide * piece
        heads = HEADS // self.peers
        self.real_cols = heads * HEAD
        self.pairs = (heads + 1) // 2
        self.cols = self.pairs * LANES
        self.tiles = self.slots // TILE


def gather_rows(geo, own, parts, column, fill):
    for back, part in enumerate(parts):
        source = lax.rem(own - back + geo.peers, geo.peers)
        for span in range(geo.wide):
            offset = pl.multiple_of(span * geo.piece + source * geo.chunk, geo.chunk)
            fill(offset, part[span, :, pl.ds(pl.multiple_of(column, LANES), LANES)])


def scatter_rows(geo, own, parts, column, source_ref):
    for back, part in enumerate(parts):
        source = lax.rem(own - back + geo.peers, geo.peers)
        for span in range(geo.wide):
            offset = pl.multiple_of(span * geo.piece + source * geo.chunk, geo.chunk)
            part[span, :, pl.ds(pl.multiple_of(column, LANES), LANES)] = source_ref[
                pl.ds(offset, geo.chunk), :
            ]


def attend_kernel(geo, table, *refs):
    peers = geo.peers
    qkv = refs[:peers]
    key_marks, query_marks = refs[peers : peers + 2]
    mixed = refs[peers + 2 : 2 * peers + 2]
    lse = refs[2 * peers + 2]
    ka, qa, vn, vt, ob = refs[2 * peers + 3 :]
    pair = pl.program_id(0)
    own = table[0]
    first = lax.broadcasted_iota(jnp.int32, (geo.chunk, LANES), 1) < HEAD

    def put_query(offset, values):
        marks = query_marks[pl.ds(offset, geo.chunk), :]
        scaled = values * 0.125
        qa[0, pl.ds(offset, geo.chunk), :] = jnp.where(first, scaled, marks)
        qa[1, pl.ds(offset, geo.chunk), :] = jnp.where(first, marks, scaled)

    def put_key(offset, values):
        marks = key_marks[pl.ds(offset, geo.chunk), :]
        ka[0, pl.ds(offset, geo.chunk), :] = jnp.where(first, values, marks)
        ka[1, pl.ds(offset, geo.chunk), :] = jnp.where(first, marks, values)

    def put_value(offset, values):
        vn[pl.ds(offset, geo.chunk), :] = values

    gather_rows(geo, own, qkv, pair * LANES, put_query)
    gather_rows(geo, own, qkv, geo.cols + pair * LANES, put_key)
    gather_rows(geo, own, qkv, 2 * geo.cols + pair * LANES, put_value)
    for tile in range(geo.tiles):
        vt[:, tile * TILE : (tile + 1) * TILE] = vn[tile * TILE : (tile + 1) * TILE, :].T

    def query_tile(tile, _):
        at = pl.multiple_of(tile * TILE, TILE)
        q0 = qa[0, pl.ds(at, TILE), :]
        q1 = qa[1, pl.ds(at, TILE), :]

        def one(q, which, step, m, l, acc):
            k = ka[which, pl.ds(step, TILE), :]
            s = dot_nt(k, q)
            m_new = jnp.maximum(m, jnp.max(s, 0, keepdims=True))
            p = jnp.exp(s - m_new)
            alpha = jnp.exp(m - m_new)
            l = l * alpha + jnp.sum(p, 0, keepdims=True)
            v = vt[which * HEAD : (which + 1) * HEAD, pl.ds(step, TILE)]
            acc = acc * alpha + dot_nn(v, p.astype(BF16))
            return m_new, l, acc

        def key_tile(index, carry):
            m0, l0, a0, m1, l1, a1 = carry
            step = pl.multiple_of(index * TILE, TILE)
            m0, l0, a0 = one(q0, 0, step, m0, l0, a0)
            m1, l1, a1 = one(q1, 1, step, m1, l1, a1)
            return m0, l0, a0, m1, l1, a1

        low = jnp.full((1, TILE), -2e30, F32)
        none = jnp.zeros((1, TILE), F32)
        blank = jnp.zeros((HEAD, TILE), F32)
        m0, l0, a0, m1, l1, a1 = lax.fori_loop(
            table[1 + tile],
            table[1 + geo.tiles + tile],
            key_tile,
            (low, none, blank, low, none, blank),
        )
        out = jnp.concatenate([a0 / l0, a1 / l1], 0)
        ob[pl.ds(at, TILE), :] = out.T.astype(BF16)
        lse[0, 0:1, pl.ds(at, TILE)] = m0 + jnp.log(l0)
        lse[0, 1:2, pl.ds(at, TILE)] = m1 + jnp.log(l1)
        return 0

    lax.fori_loop(0, geo.tiles, query_tile, 0)
    scatter_rows(geo, own, mixed, pair * LANES, ob)


def attend_back_kernel(geo, table, *refs):
    peers = geo.peers
    qkv = refs[:peers]
    grads = refs[peers : 2 * peers]
    mixed = refs[2 * peers : 3 * peers]
    lse, key_marks, query_marks, value_marks = refs[3 * peers : 3 * peers + 4]
    outs = refs[3 * peers + 4 : 4 * peers + 4]
    ka, qa, va, da, qm, dm, kn, kt, dk, dv, ob = refs[4 * peers + 4 :]
    pair = pl.program_id(0)
    own = table[0]
    lane = lax.broadcasted_iota(jnp.int32, (geo.chunk, LANES), 1)
    first = lane < HEAD
    zero = jnp.zeros((geo.chunk, LANES), BF16)

    def put_query(offset, values):
        marks = query_marks[pl.ds(offset, geo.chunk), :]
        scaled = values * 0.125
        qa[0, pl.ds(offset, geo.chunk), :] = jnp.where(first, scaled, marks)
        qa[1, pl.ds(offset, geo.chunk), :] = jnp.where(first, marks, scaled)
        qm[0, pl.ds(offset, geo.chunk), :] = jnp.where(first, scaled, zero)
        qm[1, pl.ds(offset, geo.chunk), :] = jnp.where(first, zero, scaled)

    def put_key(offset, values):
        marks = key_marks[pl.ds(offset, geo.chunk), :]
        ka[0, pl.ds(offset, geo.chunk), :] = jnp.where(first, values, marks)
        ka[1, pl.ds(offset, geo.chunk), :] = jnp.where(first, marks, values)
        kn[pl.ds(offset, geo.chunk), :] = values

    def put_value(offset, values):
        marks = value_marks[pl.ds(offset, geo.chunk), :]
        va[0, pl.ds(offset, geo.chunk), :] = jnp.where(first, values, marks)
        va[1, pl.ds(offset, geo.chunk), :] = jnp.where(first, marks, values)

    def put_mixed(offset, values):
        ob[pl.ds(offset, geo.chunk), :] = values

    def put_grad(offset, values):
        product = values.astype(F32) * ob[pl.ds(offset, geo.chunk), :].astype(F32)
        inner0 = jnp.sum(jnp.where(first, product, 0.0), 1, keepdims=True)
        inner1 = jnp.sum(jnp.where(first, 0.0, product), 1, keepdims=True)

        def digits(inner, base):
            high = (-inner).astype(BF16)
            rest = -inner - high.astype(F32)
            middle = rest.astype(BF16)
            last = (rest - middle.astype(F32)).astype(BF16)
            spread = jnp.where(
                lane == base,
                high.astype(F32),
                jnp.where(
                    lane == base + 1,
                    middle.astype(F32),
                    jnp.where(lane == base + 2, last.astype(F32), 0.0),
                ),
            )
            return spread.astype(BF16)

        da[0, pl.ds(offset, geo.chunk), :] = jnp.where(first, values, digits(inner0, HEAD))
        da[1, pl.ds(offset, geo.chunk), :] = jnp.where(first, digits(inner1, 0), values)
        dm[0, pl.ds(offset, geo.chunk), :] = jnp.where(first, values, zero)
        dm[1, pl.ds(offset, geo.chunk), :] = jnp.where(first, zero, values)

    gather_rows(geo, own, qkv, pair * LANES, put_query)
    gather_rows(geo, own, qkv, geo.cols + pair * LANES, put_key)
    gather_rows(geo, own, qkv, 2 * geo.cols + pair * LANES, put_value)
    gather_rows(geo, own, mixed, pair * LANES, put_mixed)
    gather_rows(geo, own, grads, pair * LANES, put_grad)
    for tile in range(geo.tiles):
        kt[:, tile * TILE : (tile + 1) * TILE] = kn[tile * TILE : (tile + 1) * TILE, :].T
    dk[...] = jnp.zeros_like(dk)
    dv[...] = jnp.zeros_like(dv)

    def query_tile(tile, _):
        at = pl.multiple_of(tile * TILE, TILE)

        def one(which, step):
            s = dot_nt(ka[which, pl.ds(step, TILE), :], qa[which, pl.ds(at, TILE), :])
            p = jnp.exp(s - lse[0, which : which + 1, pl.ds(at, TILE)])
            g = dot_nt(va[which, pl.ds(step, TILE), :], da[which, pl.ds(at, TILE), :])
            ds = (p * g).astype(BF16)
            return p.astype(BF16), ds

        def key_tile(index, carry):
            a0, a1 = carry
            step = pl.multiple_of(index * TILE, TILE)
            p0, s0 = one(0, step)
            p1, s1 = one(1, step)
            dv[pl.ds(step, TILE), :] += dot_nn(p0, dm[0, pl.ds(at, TILE), :]) + dot_nn(
                p1, dm[1, pl.ds(at, TILE), :]
            )
            dk[pl.ds(step, TILE), :] += dot_nn(s0, qm[0, pl.ds(at, TILE), :]) + dot_nn(
                s1, qm[1, pl.ds(at, TILE), :]
            )
            a0 = a0 + dot_nn(kt[:HEAD, pl.ds(step, TILE)], s0)
            a1 = a1 + dot_nn(kt[HEAD:, pl.ds(step, TILE)], s1)
            return a0, a1

        blank = jnp.zeros((HEAD, TILE), F32)
        a0, a1 = lax.fori_loop(
            table[1 + tile], table[1 + geo.tiles + tile], key_tile, (blank, blank)
        )
        ob[pl.ds(at, TILE), :] = (jnp.concatenate([a0, a1], 0) * 0.125).T.astype(BF16)
        return 0

    lax.fori_loop(0, geo.tiles, query_tile, 0)
    scatter_rows(geo, own, outs, pair * LANES, ob)
    ob[...] = dk[...].astype(BF16)
    scatter_rows(geo, own, outs, geo.cols + pair * LANES, ob)
    ob[...] = dv[...].astype(BF16)
    scatter_rows(geo, own, outs, 2 * geo.cols + pair * LANES, ob)


def whole_spec(shape):
    return pl.BlockSpec(shape, lambda pair, table: (0,) * len(shape))


def attend(geo, table, qkv_parts, key_marks, query_marks):
    out_shape = [
        jax.ShapeDtypeStruct((geo.wide, geo.chunk, geo.cols), BF16) for _ in range(geo.peers)
    ] + [jax.ShapeDtypeStruct((geo.pairs, 8, geo.slots), F32)]
    return pl.pallas_call(
        functools.partial(attend_kernel, geo),
        name="attend",
        out_shape=out_shape,
        grid_spec=pltpu.PrefetchScalarGridSpec(
            num_scalar_prefetch=1,
            grid=(geo.pairs,),
            in_specs=[whole_spec(a.shape) for a in qkv_parts]
            + [whole_spec((geo.slots, LANES))] * 2,
            out_specs=[whole_spec((geo.wide, geo.chunk, geo.cols))] * geo.peers
            + [pl.BlockSpec((1, 8, geo.slots), lambda pair, table: (pair, 0, 0))],
            scratch_shapes=[
                pltpu.VMEM((2, geo.slots, LANES), BF16),
                pltpu.VMEM((2, geo.slots, LANES), BF16),
                pltpu.VMEM((geo.slots, LANES), BF16),
                pltpu.VMEM((LANES, geo.slots), BF16),
                pltpu.VMEM((geo.slots, LANES), BF16),
            ],
        ),
        cost_estimate=pl.CostEstimate(
            flops=4 * geo.slots * geo.slots * geo.real_cols,
            transcendentals=geo.slots * geo.slots * 6,
            bytes_accessed=4 * geo.slots * geo.cols * 2,
        ),
    )(table, *qkv_parts, key_marks, query_marks)


def attend_back(geo, table, qkv_parts, grad_parts, mixed_parts, lse, key_marks, query_marks, value_marks):
    wide_shape = (geo.wide, geo.chunk, 3 * geo.cols)
    two = pltpu.VMEM((2, geo.slots, LANES), BF16)
    return pl.pallas_call(
        functools.partial(attend_back_kernel, geo),
        name="attend_back",
        out_shape=[jax.ShapeDtypeStruct(wide_shape, BF16) for _ in range(geo.peers)],
        grid_spec=pltpu.PrefetchScalarGridSpec(
            num_scalar_prefetch=1,
            grid=(geo.pairs,),
            in_specs=[whole_spec(a.shape) for a in (*qkv_parts, *grad_parts, *mixed_parts)]
            + [pl.BlockSpec((1, 8, geo.slots), lambda pair, table: (pair, 0, 0))]
            + [whole_spec((geo.slots, LANES))] * 3,
            out_specs=[whole_spec(wide_shape)] * geo.peers,
            scratch_shapes=[two] * 6
            + [
                pltpu.VMEM((geo.slots, LANES), BF16),
                pltpu.VMEM((LANES, geo.slots), BF16),
                pltpu.VMEM((geo.slots, LANES), F32),
                pltpu.VMEM((geo.slots, LANES), F32),
                pltpu.VMEM((geo.slots, LANES), BF16),
            ],
        ),
        cost_estimate=pl.CostEstimate(
            flops=10 * geo.slots * geo.slots * geo.real_cols,
            transcendentals=geo.slots * geo.slots * 6,
            bytes_accessed=12 * geo.slots * geo.cols * 2,
        ),
    )(table, *qkv_parts, *grad_parts, *mixed_parts, lse, key_marks, query_marks, value_marks)


def marks_of(block_ids, geo):
    lane = lax.broadcasted_iota(jnp.int32, (geo.slots, LANES), 1) % HEAD
    number = block_ids[:, None] + 1
    key_marks = (lane == number).astype(BF16)
    query_marks = jnp.where((lane < 9) & (lane != number), FAR, 0.0).astype(BF16)
    value_marks = (lane < 3).astype(BF16)
    return key_marks, query_marks, value_marks


def tile_table(block_ids, own, geo):
    ids = block_ids.reshape(geo.tiles, TILE, 1)
    present = jnp.any(ids == jnp.arange(-1, 8, dtype=jnp.int32), 1)
    shared = jnp.any(present[:, None] & present[None], -1)
    places = jnp.arange(geo.tiles, dtype=jnp.int32)
    low = jnp.min(jnp.where(shared, places, geo.tiles), 1)
    high = jnp.max(jnp.where(shared, places + 1, 0), 1)
    return jnp.concatenate([own[None], low, high]).astype(jnp.int32)


def pick(parts, own, target):
    peers = len(parts)
    result = parts[0]
    for step in range(1, peers):
        result = jnp.where((target - own + peers) % peers == step, parts[step], result)
    return result


def ahead(wide, peers, step):
    return [(w, w // peers * peers + (w % peers + step) % peers) for w in range(wide)]


def per_device(
    tokens,
    segment_ids,
    cotangent,
    w_qkv,
    b_qv,
    w_out,
    b_out,
    ls_attn,
    ln1_gain,
    ln1_bias,
    ln2_gain,
    ln2_bias,
    w_fc1,
    b_fc1,
    w_fc2,
    b_fc2,
    ls_mlp,
):
    geo = Geometry(lax.axis_size("wide"), tokens.shape[3])
    wide, peers, chunk, rows, cols = geo.wide, geo.peers, geo.chunk, geo.rows, geo.cols
    own = lax.axis_index("wide") % peers

    def regroup(array):
        return lax.all_to_all(array, "wide", split_axis=0, concat_axis=0, tiled=True)

    ids_out = jnp.broadcast_to(segment_ids.reshape(GROUPS, 1, geo.piece), (GROUPS, peers, geo.piece))
    block_ids = regroup(ids_out.reshape(wide, geo.piece)).reshape(geo.slots)
    token_rows = regroup(tokens.reshape(wide, chunk, D)).reshape(rows, D)
    cotangent, token_rows = lax.optimization_barrier((cotangent, token_rows))
    cotangent_rows = regroup(cotangent.reshape(wide, chunk, D)).reshape(rows, D)

    my_ids = lax.dynamic_index_in_dim(
        block_ids.reshape(wide, peers, chunk), own, 1, keepdims=False
    ).reshape(rows, 1)
    valid_rows = (my_ids >= 0).astype(F32)
    key_marks, query_marks, value_marks = marks_of(block_ids, geo)
    table = tile_table(block_ids, own, geo)

    bias_all = jnp.concatenate([b_qv[:D], jnp.zeros((D,), F32), b_qv[D:]])
    w_heads = w_qkv.reshape(D, 3, peers, geo.real_cols)
    b_heads = bias_all.reshape(3, peers, geo.real_cols)
    o_heads = w_out.reshape(peers, geo.real_cols, D)
    spare = cols - geo.real_cols

    def heads_of(step):
        group = (own + step) % peers
        w = lax.dynamic_index_in_dim(w_heads, group, 2, keepdims=False)
        b = lax.dynamic_index_in_dim(b_heads, group, 1, keepdims=False)
        o = lax.dynamic_index_in_dim(o_heads, group, 0, keepdims=False)
        w = jnp.pad(w, ((0, 0), (0, 0), (0, spare))).reshape(D, 3 * cols)
        b = jnp.pad(b, ((0, 0), (0, spare))).reshape(3 * cols)
        return w, b, jnp.pad(o, ((0, spare), (0, 0)))

    weights = [heads_of(step) for step in range(peers)]

    def send(array, step):
        return lax.ppermute(array, "wide", ahead(wide, peers, step % peers))

    inputs = token_rows.astype(F32)
    normed, norm_first_back = jax.vjp(layer_norm, inputs, ln1_gain, ln1_bias)
    normed_low = normed.astype(BF16)
    qkv_parts = [None] * peers
    for step in [*range(1, peers), 0]:
        w, b, _ = weights[step]
        made = (dot_nn(normed_low, w) + b).astype(BF16).reshape(wide, chunk, 3 * cols)
        qkv_parts[step] = send(made, step) if step else made
    *mixed_parts, lse = attend(geo, table, qkv_parts, key_marks, query_marks)
    mixed_home = [
        (send(part, -step) if step else part).reshape(rows, cols)
        for step, part in enumerate(mixed_parts)
    ]
    mixed_rows = jnp.concatenate(mixed_home, 1)
    w_out_rel = jnp.concatenate([o for _, _, o in weights], 0)
    projected = dot_nn(mixed_rows, w_out_rel) + b_out
    hidden = inputs + ls_attn * projected
    second, norm_second_back = jax.vjp(layer_norm, hidden, ln2_gain, ln2_bias)
    second_low = second.astype(BF16)
    pre_act = dot_nn(second_low, w_fc1) + b_fc1
    activation, gelu_back = jax.vjp(gelu_exact, pre_act)
    act_low = activation.astype(BF16)
    mlp_out = dot_nn(act_low, w_fc2) + b_fc2
    result = ((hidden + ls_mlp * mlp_out) * valid_rows).astype(BF16)
    output = regroup(result.reshape(wide, chunk, D)).reshape(tokens.shape)
    grad_out = cotangent_rows.astype(F32) * valid_rows
    grad_ls_mlp = jnp.sum(grad_out * mlp_out, 0)
    grad_mlp = (ls_mlp * grad_out).astype(BF16)
    grad_b_fc2 = jnp.sum(grad_mlp.astype(F32), 0)
    grad_w_fc2 = jnp.einsum("tf,td->fd", act_low, grad_mlp, preferred_element_type=F32)
    grad_act = jnp.dot(grad_mlp, w_fc2.T, preferred_element_type=F32)
    grad_pre = gelu_back(grad_act)[0].astype(BF16)
    grad_b_fc1 = jnp.sum(grad_pre.astype(F32), 0)
    grad_w_fc1 = jnp.einsum("td,tf->df", second_low, grad_pre, preferred_element_type=F32)
    grad_second = jnp.dot(grad_pre, w_fc1.T, preferred_element_type=F32)
    grad_hidden_norm, grad_ln2_gain, grad_ln2_bias = norm_second_back(grad_second)
    grad_hidden = grad_out + grad_hidden_norm
    grad_ls_attn = jnp.sum(grad_hidden * projected, 0)
    grad_proj = (ls_attn * grad_hidden).astype(BF16)
    grad_b_out = jnp.sum(grad_proj.astype(F32), 0)
    grad_parts = [None] * peers
    for step in [*range(1, peers), 0]:
        made = jnp.dot(grad_proj, weights[step][2].T, preferred_element_type=F32)
        made = made.astype(BF16).reshape(wide, chunk, cols)
        grad_parts[step] = send(made, step) if step else made
    grad_w_out_rel = jnp.einsum("td,te->de", mixed_rows, grad_proj, preferred_element_type=F32)
    grad_w_out_parts = [
        grad_w_out_rel[step * cols : step * cols + geo.real_cols].astype(BF16)
        for step in range(peers)
    ]
    grad_w_out = jnp.concatenate([pick(grad_w_out_parts, own, g) for g in range(peers)], 0)

    dqkv_parts = attend_back(
        geo, table, qkv_parts, grad_parts, mixed_parts, lse, key_marks, query_marks, value_marks
    )
    dqkv_home = [
        (send(part, -step) if step else part).reshape(rows, 3 * cols)
        for step, part in enumerate(dqkv_parts)
    ]
    grad_qkv = jnp.concatenate(dqkv_home, 1)
    w_qkv_rel = jnp.concatenate([w for w, _, _ in weights], 1)
    grad_normed = jnp.dot(grad_qkv, w_qkv_rel.T, preferred_element_type=F32)
    sums_rel = jnp.sum(grad_qkv.astype(F32), 0).reshape(peers, 3, cols)[:, :, : geo.real_cols]
    sums = jnp.stack([pick(list(sums_rel), own, g) for g in range(peers)], 1).reshape(3, D)
    grad_b_qv = jnp.concatenate([sums[0], sums[2]])
    grad_w_rel = jnp.einsum("td,te->de", normed_low, grad_qkv, preferred_element_type=F32)
    grad_w_rel = grad_w_rel.astype(BF16).reshape(D, peers, 3, cols)[..., : geo.real_cols]
    grad_w_qkv = jnp.stack(
        [pick([grad_w_rel[:, k] for k in range(peers)], own, g) for g in range(peers)], 2
    ).reshape(D, 3 * D)
    grad_inputs_norm, grad_ln1_gain, grad_ln1_bias = norm_first_back(grad_normed)
    grad_tokens = regroup(
        (grad_hidden + grad_inputs_norm).astype(BF16).reshape(wide, chunk, D)
    ).reshape(tokens.shape)

    def reduced(array):
        share = lax.psum_scatter(array.astype(BF16), "narrow", scatter_dimension=0, tiled=True)
        return lax.psum(share, "wide").astype(F32)

    narrow = lax.axis_size("narrow")
    vectors = [
        grad_b_qv,
        grad_b_out,
        grad_ls_attn,
        grad_ln1_gain,
        grad_ln1_bias,
        grad_ln2_gain,
        grad_ln2_bias,
        grad_b_fc1,
        grad_b_fc2,
        grad_ls_mlp,
    ]
    packed = jnp.concatenate([v.reshape(narrow, -1) for v in vectors], 1)
    packed = lax.psum_scatter(packed, "narrow", scatter_dimension=0, tiled=False)
    packed = lax.psum(packed, "wide")
    small, start = [], 0
    for v in vectors:
        size = v.shape[0] // narrow
        small.append(packed[start : start + size])
        start += size
    return (
        output,
        grad_tokens,
        reduced(grad_w_qkv),
        small[0],
        reduced(grad_w_out),
        small[1],
        small[2],
        small[3],
        small[4],
        small[5],
        small[6],
        reduced(grad_w_fc1),
        small[7],
        reduced(grad_w_fc2),
        small[8],
        small[9],
    )


def solution(mesh):
    rows = P("narrow", "wide", None, None, None)
    placed = (rows, P("narrow", "wide", None, None), rows) + (P(),) * 14
    matrix, vector = P("narrow", None), P("narrow")
    return jax.shard_map(
        per_device,
        mesh=mesh,
        in_specs=placed,
        out_specs=(
            rows,
            rows,
            matrix,
            vector,
            matrix,
            vector,
            vector,
            vector,
            vector,
            vector,
            vector,
            matrix,
            vector,
            matrix,
            vector,
            vector,
        ),
        check_vma=False,
    )
```

```python
import functools
import jax
import jax.numpy as jnp
from jax import lax
from jax.experimental import pallas as pl
from jax.experimental.pallas import tpu as pltpu
from jax.sharding import PartitionSpec as P

D = 768
HEADS = 12
HEAD = 64
GROUPS = 4
TILE = 512
KEYS = 512
LANES = 128
EPSILON = 1e-06
ROOT_HALF = 0.7071067811865476
FAR = -1e30
F32 = jnp.float32
BF16 = jnp.bfloat16


def layer_norm(values, gain, bias):
    average = jnp.mean(values, -1, keepdims=True)
    centred = values - average
    variance = jnp.mean(centred * centred, -1, keepdims=True)
    return centred * lax.rsqrt(variance + EPSILON) * gain + bias


def gelu_exact(values):
    return 0.5 * values * (1.0 + lax.erf(values * ROOT_HALF))


def dot_nt(a, b):
    return lax.dot_general(a, b, (((1,), (1,)), ((), ())), preferred_element_type=F32)


def dot_nn(a, b):
    return jnp.dot(a, b, preferred_element_type=F32)


class Geometry:
    def __init__(self, wide, piece):
        self.wide = wide
        self.piece = piece
        self.peers = wide // GROUPS
        self.chunk = piece // self.peers
        self.rows = wide * self.chunk
        self.slots = wide * piece
        heads = HEADS // self.peers
        self.real_cols = heads * HEAD
        self.pairs = (heads + 1) // 2
        self.cols = self.pairs * LANES
        self.tiles = self.slots // TILE


def gather_rows(geo, own, parts, column, fill):
    for back, part in enumerate(parts):
        source = lax.rem(own - back + geo.peers, geo.peers)
        for span in range(geo.wide):
            offset = pl.multiple_of(span * geo.piece + source * geo.chunk, geo.chunk)
            fill(offset, part[span, :, pl.ds(pl.multiple_of(column, LANES), LANES)])


def scatter_rows(geo, own, parts, column, source_ref):
    for back, part in enumerate(parts):
        source = lax.rem(own - back + geo.peers, geo.peers)
        for span in range(geo.wide):
            offset = pl.multiple_of(span * geo.piece + source * geo.chunk, geo.chunk)
            part[span, :, pl.ds(pl.multiple_of(column, LANES), LANES)] = source_ref[
                pl.ds(offset, geo.chunk), :
            ]


def attend_kernel(geo, table, *refs):
    peers = geo.peers
    qkv = refs[:peers]
    key_marks, query_marks = refs[peers : peers + 2]
    mixed = refs[peers + 2 : 2 * peers + 2]
    lse = refs[2 * peers + 2]
    ka, qa, va, ob, worst = refs[2 * peers + 3 :]
    pair = pl.program_id(0)
    own = table[0]
    first = lax.broadcasted_iota(jnp.int32, (geo.chunk, LANES), 1) < HEAD
    left = lax.broadcasted_iota(jnp.int32, (TILE, LANES), 1) < HEAD
    one = jnp.ones((geo.chunk, LANES), BF16)
    picks = lax.broadcasted_iota(jnp.int32, (8, LANES), 1) == HEAD * lax.broadcasted_iota(
        jnp.int32, (8, LANES), 0
    )

    def put_query(offset, values):
        marks = query_marks[pl.ds(offset, geo.chunk), :]
        scaled = values * 0.125
        qa[0, pl.ds(offset, geo.chunk), :] = jnp.where(first, scaled, marks)
        qa[1, pl.ds(offset, geo.chunk), :] = jnp.where(first, marks, scaled)

    def put_key(offset, values):
        marks = key_marks[pl.ds(offset, geo.chunk), :]
        ka[0, pl.ds(offset, geo.chunk), :] = jnp.where(first, values, marks)
        ka[1, pl.ds(offset, geo.chunk), :] = jnp.where(first, marks, values)

    def put_value(offset, values):
        va[0, pl.ds(offset, geo.chunk), :] = jnp.where(first, values, one)
        va[1, pl.ds(offset, geo.chunk), :] = jnp.where(first, one, values)

    gather_rows(geo, own, qkv, pair * LANES, put_query)
    gather_rows(geo, own, qkv, geo.cols + pair * LANES, put_key)
    gather_rows(geo, own, qkv, 2 * geo.cols + pair * LANES, put_value)

    def scores(which, step, at):
        return dot_nt(qa[which, pl.ds(at, TILE), :], ka[which, pl.ds(step, KEYS), :])

    def weighted(which, step, p):
        return dot_nn(p.astype(BF16), va[which, pl.ds(step, KEYS), :])

    def store(at, acc0, acc1, m0, m1):
        totals = pltpu.roll(jnp.where(left, acc1, acc0), HEAD, 1)
        ob[pl.ds(at, TILE), :] = (jnp.where(left, acc0, acc1) / totals).astype(BF16)
        logs = jnp.log(totals) + jnp.where(left, m0, m1)
        lse[0, :, pl.ds(at, TILE)] = lax.dot_general(
            picks.astype(F32),
            logs,
            (((1,), (1,)), ((), ())),
            precision=lax.Precision.HIGHEST,
            preferred_element_type=F32,
        )
        return totals

    def plain_tile(tile, _):
        at = pl.multiple_of(tile * TILE, TILE)

        def key_tile(index, carry):
            acc0, acc1 = carry
            step = pl.multiple_of(index * KEYS, KEYS)
            p0 = jnp.exp(scores(0, step, at))
            p1 = jnp.exp(scores(1, step, at))
            return acc0 + weighted(0, step, p0), acc1 + weighted(1, step, p1)

        blank = jnp.zeros((TILE, LANES), F32)
        acc0, acc1 = lax.fori_loop(
            table[1 + tile], table[1 + geo.tiles + tile], key_tile, (blank, blank)
        )
        totals = store(at, acc0, acc1, 0.0, 0.0)
        odd = jnp.where((totals > 1e-20) & (totals < 1e20), 0.0, 1.0)
        worst[...] = jnp.maximum(worst[...], jnp.max(odd.reshape(TILE // 8, 8, LANES), 0))
        return 0

    def careful_tile(tile, _):
        at = pl.multiple_of(tile * TILE, TILE)

        def one_head(which, step, m, acc):
            s = scores(which, step, at)
            m_new = jnp.maximum(m, jnp.max(s, 1, keepdims=True))
            acc = acc * jnp.exp(m - m_new) + weighted(which, step, jnp.exp(s - m_new))
            return m_new, acc

        def key_tile(index, carry):
            step = pl.multiple_of(index * KEYS, KEYS)
            return (*one_head(0, step, *carry[:2]), *one_head(1, step, *carry[2:]))

        low = jnp.full((TILE, 1), -2e30, F32)
        blank = jnp.zeros((TILE, LANES), F32)
        m0, acc0, m1, acc1 = lax.fori_loop(
            table[1 + tile], table[1 + geo.tiles + tile], key_tile, (low, blank, low, blank)
        )
        store(at, acc0, acc1, m0, m1)
        return 0

    worst[...] = jnp.zeros_like(worst)
    lax.fori_loop(0, geo.tiles, plain_tile, 0)

    @pl.when(jnp.max(worst[...]) > 0.0)
    def _():
        lax.fori_loop(0, geo.tiles, careful_tile, 0)

    scatter_rows(geo, own, mixed, pair * LANES, ob)


def attend_back_kernel(geo, table, *refs):
    peers = geo.peers
    qkv = refs[:peers]
    grads = refs[peers : 2 * peers]
    mixed = refs[2 * peers : 3 * peers]
    lse, key_marks, query_marks = refs[3 * peers : 3 * peers + 3]
    outs = refs[3 * peers + 3 : 4 * peers + 3]
    ka, qa, vn, qm, dm, kn, kt, dk, dv, ob, inner = refs[4 * peers + 3 :]
    pair = pl.program_id(0)
    own = table[0]
    lane = lax.broadcasted_iota(jnp.int32, (geo.chunk, LANES), 1)
    first = lane < HEAD
    zero = jnp.zeros((geo.chunk, LANES), BF16)
    half = lax.broadcasted_iota(jnp.int32, (8, LANES), 1) // HEAD == lax.broadcasted_iota(
        jnp.int32, (8, LANES), 0
    )
    half = half.astype(BF16)

    def put_query(offset, values):
        marks = query_marks[pl.ds(offset, geo.chunk), :]
        scaled = values * 0.125
        qa[0, pl.ds(offset, geo.chunk), :] = jnp.where(first, scaled, marks)
        qa[1, pl.ds(offset, geo.chunk), :] = jnp.where(first, marks, scaled)
        qm[0, pl.ds(offset, geo.chunk), :] = jnp.where(first, scaled, zero)
        qm[1, pl.ds(offset, geo.chunk), :] = jnp.where(first, zero, scaled)

    def put_key(offset, values):
        marks = key_marks[pl.ds(offset, geo.chunk), :]
        ka[0, pl.ds(offset, geo.chunk), :] = jnp.where(first, values, marks)
        ka[1, pl.ds(offset, geo.chunk), :] = jnp.where(first, marks, values)
        kn[pl.ds(offset, geo.chunk), :] = values

    def put_value(offset, values):
        vn[pl.ds(offset, geo.chunk), :] = values

    def put_mixed(offset, values):
        ob[pl.ds(offset, geo.chunk), :] = values

    def put_grad(offset, values):
        dm[0, pl.ds(offset, geo.chunk), :] = jnp.where(first, values, zero)
        dm[1, pl.ds(offset, geo.chunk), :] = jnp.where(first, zero, values)
        product = values.astype(F32) * ob[pl.ds(offset, geo.chunk), :].astype(F32)
        high = product.astype(BF16)
        rest = (product - high.astype(F32)).astype(BF16)
        kn[pl.ds(offset, geo.chunk), :] = high
        vn[pl.ds(offset, geo.chunk), :] = rest

    gather_rows(geo, own, mixed, pair * LANES, put_mixed)
    gather_rows(geo, own, grads, pair * LANES, put_grad)
    for tile in range(geo.tiles):
        rows = slice(tile * TILE, (tile + 1) * TILE)
        inner[:, rows] = dot_nt(half, kn[rows, :]) + dot_nt(half, vn[rows, :])
    gather_rows(geo, own, qkv, pair * LANES, put_query)
    gather_rows(geo, own, qkv, geo.cols + pair * LANES, put_key)
    gather_rows(geo, own, qkv, 2 * geo.cols + pair * LANES, put_value)
    for tile in range(geo.tiles):
        rows = slice(tile * TILE, (tile + 1) * TILE)
        kt[:, rows] = kn[rows, :].T
    dk[...] = jnp.zeros_like(dk)
    dv[...] = jnp.zeros_like(dv)

    def query_tile(tile, _):
        at = pl.multiple_of(tile * TILE, TILE)

        def one(which, step):
            s = dot_nt(ka[which, pl.ds(step, KEYS), :], qa[which, pl.ds(at, TILE), :])
            p = jnp.exp(s - lse[0, which : which + 1, pl.ds(at, TILE)])
            g = dot_nt(vn[pl.ds(step, KEYS), :], dm[which, pl.ds(at, TILE), :])
            ds = (p * (g - inner[which : which + 1, pl.ds(at, TILE)])).astype(BF16)
            return p.astype(BF16), ds

        def key_tile(index, carry):
            a0, a1 = carry
            step = pl.multiple_of(index * KEYS, KEYS)
            p0, s0 = one(0, step)
            p1, s1 = one(1, step)
            dv[pl.ds(step, KEYS), :] += dot_nn(p0, dm[0, pl.ds(at, TILE), :]) + dot_nn(
                p1, dm[1, pl.ds(at, TILE), :]
            )
            dk[pl.ds(step, KEYS), :] += dot_nn(s0, qm[0, pl.ds(at, TILE), :]) + dot_nn(
                s1, qm[1, pl.ds(at, TILE), :]
            )
            a0 = a0 + dot_nn(kt[:HEAD, pl.ds(step, KEYS)], s0)
            a1 = a1 + dot_nn(kt[HEAD:, pl.ds(step, KEYS)], s1)
            return a0, a1

        blank = jnp.zeros((HEAD, TILE), F32)
        a0, a1 = lax.fori_loop(
            table[1 + tile], table[1 + geo.tiles + tile], key_tile, (blank, blank)
        )
        ob[pl.ds(at, TILE), :] = (jnp.concatenate([a0, a1], 0) * 0.125).T.astype(BF16)
        return 0

    lax.fori_loop(0, geo.tiles, query_tile, 0)
    scatter_rows(geo, own, outs, pair * LANES, ob)
    ob[...] = dk[...].astype(BF16)
    scatter_rows(geo, own, outs, geo.cols + pair * LANES, ob)
    ob[...] = dv[...].astype(BF16)
    scatter_rows(geo, own, outs, 2 * geo.cols + pair * LANES, ob)


def whole_spec(shape):
    return pl.BlockSpec(shape, lambda pair, table: (0,) * len(shape))


def attend(geo, table, qkv_parts, key_marks, query_marks):
    out_shape = [
        jax.ShapeDtypeStruct((geo.wide, geo.chunk, geo.cols), BF16) for _ in range(geo.peers)
    ] + [jax.ShapeDtypeStruct((geo.pairs, 8, geo.slots), F32)]
    return pl.pallas_call(
        functools.partial(attend_kernel, geo),
        name="attend",
        out_shape=out_shape,
        grid_spec=pltpu.PrefetchScalarGridSpec(
            num_scalar_prefetch=1,
            grid=(geo.pairs,),
            in_specs=[whole_spec(a.shape) for a in qkv_parts]
            + [whole_spec((geo.slots, LANES))] * 2,
            out_specs=[whole_spec((geo.wide, geo.chunk, geo.cols))] * geo.peers
            + [pl.BlockSpec((1, 8, geo.slots), lambda pair, table: (pair, 0, 0))],
            scratch_shapes=[
                pltpu.VMEM((2, geo.slots, LANES), BF16),
                pltpu.VMEM((2, geo.slots, LANES), BF16),
                pltpu.VMEM((2, geo.slots, LANES), BF16),
                pltpu.VMEM((geo.slots, LANES), BF16),
                pltpu.VMEM((8, LANES), F32),
            ],
        ),
        cost_estimate=pl.CostEstimate(
            flops=4 * geo.slots * geo.slots * geo.real_cols,
            transcendentals=geo.slots * geo.slots * 6,
            bytes_accessed=4 * geo.slots * geo.cols * 2,
        ),
    )(table, *qkv_parts, key_marks, query_marks)


def attend_back(geo, table, qkv_parts, grad_parts, mixed_parts, lse, key_marks, query_marks):
    wide_shape = (geo.wide, geo.chunk, 3 * geo.cols)
    two = pltpu.VMEM((2, geo.slots, LANES), BF16)
    one = pltpu.VMEM((geo.slots, LANES), BF16)
    return pl.pallas_call(
        functools.partial(attend_back_kernel, geo),
        name="attend_back",
        out_shape=[jax.ShapeDtypeStruct(wide_shape, BF16) for _ in range(geo.peers)],
        grid_spec=pltpu.PrefetchScalarGridSpec(
            num_scalar_prefetch=1,
            grid=(geo.pairs,),
            in_specs=[whole_spec(a.shape) for a in (*qkv_parts, *grad_parts, *mixed_parts)]
            + [pl.BlockSpec((1, 8, geo.slots), lambda pair, table: (pair, 0, 0))]
            + [whole_spec((geo.slots, LANES))] * 2,
            out_specs=[whole_spec(wide_shape)] * geo.peers,
            scratch_shapes=[two, two, one, two, two, one]
            + [
                pltpu.VMEM((LANES, geo.slots), BF16),
                pltpu.VMEM((geo.slots, LANES), F32),
                pltpu.VMEM((geo.slots, LANES), F32),
                one,
                pltpu.VMEM((8, geo.slots), F32),
            ],
        ),
        cost_estimate=pl.CostEstimate(
            flops=10 * geo.slots * geo.slots * geo.real_cols,
            transcendentals=geo.slots * geo.slots * 6,
            bytes_accessed=12 * geo.slots * geo.cols * 2,
        ),
    )(table, *qkv_parts, *grad_parts, *mixed_parts, lse, key_marks, query_marks)


def marks_of(block_ids, geo):
    lane = lax.broadcasted_iota(jnp.int32, (geo.slots, LANES), 1) % HEAD
    number = block_ids[:, None] + 1
    key_marks = (lane == number).astype(BF16)
    query_marks = jnp.where((lane < 9) & (lane != number), FAR, 0.0).astype(BF16)
    return key_marks, query_marks


def tile_table(block_ids, own, geo):
    def present(size):
        return jnp.any(block_ids.reshape(-1, size, 1) == jnp.arange(-1, 8, dtype=jnp.int32), 1)

    shared = jnp.any(present(TILE)[:, None] & present(KEYS)[None], -1)
    places = jnp.arange(geo.slots // KEYS, dtype=jnp.int32)
    low = jnp.min(jnp.where(shared, places, geo.tiles), 1)
    high = jnp.max(jnp.where(shared, places + 1, 0), 1)
    return jnp.concatenate([own[None], low, high]).astype(jnp.int32)


def pick(parts, own, target):
    peers = len(parts)
    result = parts[0]
    for step in range(1, peers):
        result = jnp.where((target - own + peers) % peers == step, parts[step], result)
    return result


def ahead(wide, peers, step):
    return [(w, w // peers * peers + (w % peers + step) % peers) for w in range(wide)]


def per_device(
    tokens,
    segment_ids,
    cotangent,
    w_qkv,
    b_qv,
    w_out,
    b_out,
    ls_attn,
    ln1_gain,
    ln1_bias,
    ln2_gain,
    ln2_bias,
    w_fc1,
    b_fc1,
    w_fc2,
    b_fc2,
    ls_mlp,
):
    geo = Geometry(lax.axis_size("wide"), tokens.shape[3])
    wide, peers, chunk, rows, cols = geo.wide, geo.peers, geo.chunk, geo.rows, geo.cols
    own = lax.axis_index("wide") % peers

    def regroup(array):
        return lax.all_to_all(array, "wide", split_axis=0, concat_axis=0, tiled=True)

    ids_out = jnp.broadcast_to(segment_ids.reshape(GROUPS, 1, geo.piece), (GROUPS, peers, geo.piece))
    block_ids = regroup(ids_out.reshape(wide, geo.piece)).reshape(geo.slots)
    token_rows = regroup(tokens.reshape(wide, chunk, D)).reshape(rows, D)
    cotangent, token_rows = lax.optimization_barrier((cotangent, token_rows))
    cotangent_rows = regroup(cotangent.reshape(wide, chunk, D)).reshape(rows, D)

    my_ids = lax.dynamic_index_in_dim(
        block_ids.reshape(wide, peers, chunk), own, 1, keepdims=False
    ).reshape(rows, 1)
    valid_rows = (my_ids >= 0).astype(F32)
    key_marks, query_marks = marks_of(block_ids, geo)
    table = tile_table(block_ids, own, geo)

    bias_all = jnp.concatenate([b_qv[:D], jnp.zeros((D,), F32), b_qv[D:]])
    w_heads = w_qkv.reshape(D, 3, peers, geo.real_cols)
    b_heads = bias_all.reshape(3, peers, geo.real_cols)
    o_heads = w_out.reshape(peers, geo.real_cols, D)
    spare = cols - geo.real_cols

    def heads_of(step):
        group = (own + step) % peers
        w = lax.dynamic_index_in_dim(w_heads, group, 2, keepdims=False)
        b = lax.dynamic_index_in_dim(b_heads, group, 1, keepdims=False)
        o = lax.dynamic_index_in_dim(o_heads, group, 0, keepdims=False)
        w = jnp.pad(w, ((0, 0), (0, 0), (0, spare))).reshape(D, 3 * cols)
        b = jnp.pad(b, ((0, 0), (0, spare))).reshape(3 * cols)
        return w, b, jnp.pad(o, ((0, spare), (0, 0)))

    weights = [heads_of(step) for step in range(peers)]

    def send(array, step):
        return lax.ppermute(array, "wide", ahead(wide, peers, step % peers))

    inputs = token_rows.astype(F32)
    normed, norm_first_back = jax.vjp(layer_norm, inputs, ln1_gain, ln1_bias)
    normed_low = normed.astype(BF16)
    qkv_parts = [None] * peers
    for step in [*range(1, peers), 0]:
        w, b, _ = weights[step]
        made = (dot_nn(normed_low, w) + b).astype(BF16).reshape(wide, chunk, 3 * cols)
        qkv_parts[step] = send(made, step) if step else made
    *mixed_parts, lse = attend(geo, table, qkv_parts, key_marks, query_marks)
    mixed_home = [
        (send(part, -step) if step else part).reshape(rows, cols)
        for step, part in enumerate(mixed_parts)
    ]
    mixed_rows = jnp.concatenate(mixed_home, 1)
    w_out_rel = jnp.concatenate([o for _, _, o in weights], 0)
    projected = dot_nn(mixed_rows, w_out_rel) + b_out
    hidden = inputs + ls_attn * projected
    second, norm_second_back = jax.vjp(layer_norm, hidden, ln2_gain, ln2_bias)
    second_low = second.astype(BF16)
    pre_act = dot_nn(second_low, w_fc1) + b_fc1
    activation, gelu_back = jax.vjp(gelu_exact, pre_act)
    act_low = activation.astype(BF16)
    mlp_out = dot_nn(act_low, w_fc2) + b_fc2
    result = ((hidden + ls_mlp * mlp_out) * valid_rows).astype(BF16)
    output = regroup(result.reshape(wide, chunk, D)).reshape(tokens.shape)
    grad_out = cotangent_rows.astype(F32) * valid_rows
    grad_ls_mlp = jnp.sum(grad_out * mlp_out, 0)
    grad_mlp = (ls_mlp * grad_out).astype(BF16)
    grad_b_fc2 = jnp.sum(grad_mlp.astype(F32), 0)
    grad_w_fc2 = jnp.einsum("tf,td->fd", act_low, grad_mlp, preferred_element_type=F32)
    grad_act = jnp.dot(grad_mlp, w_fc2.T, preferred_element_type=F32)
    grad_pre = gelu_back(grad_act)[0].astype(BF16)
    grad_b_fc1 = jnp.sum(grad_pre.astype(F32), 0)
    grad_w_fc1 = jnp.einsum("td,tf->df", second_low, grad_pre, preferred_element_type=F32)
    grad_second = jnp.dot(grad_pre, w_fc1.T, preferred_element_type=F32)
    grad_hidden_norm, grad_ln2_gain, grad_ln2_bias = norm_second_back(grad_second)
    grad_hidden = grad_out + grad_hidden_norm
    grad_ls_attn = jnp.sum(grad_hidden * projected, 0)
    grad_proj = (ls_attn * grad_hidden).astype(BF16)
    grad_b_out = jnp.sum(grad_proj.astype(F32), 0)
    grad_parts = [None] * peers
    for step in [*range(1, peers), 0]:
        made = jnp.dot(grad_proj, weights[step][2].T, preferred_element_type=F32)
        made = made.astype(BF16).reshape(wide, chunk, cols)
        grad_parts[step] = send(made, step) if step else made
    grad_w_out_rel = jnp.einsum("td,te->de", mixed_rows, grad_proj, preferred_element_type=F32)
    grad_w_out_parts = [
        grad_w_out_rel[step * cols : step * cols + geo.real_cols].astype(BF16)
        for step in range(peers)
    ]
    grad_w_out = jnp.concatenate([pick(grad_w_out_parts, own, g) for g in range(peers)], 0)

    dqkv_parts = attend_back(
        geo, table, qkv_parts, grad_parts, mixed_parts, lse, key_marks, query_marks
    )
    dqkv_home = [
        (send(part, -step) if step else part).reshape(rows, 3 * cols)
        for step, part in enumerate(dqkv_parts)
    ]
    grad_qkv = jnp.concatenate(dqkv_home, 1)
    w_qkv_rel = jnp.concatenate([w for w, _, _ in weights], 1)
    grad_normed = jnp.dot(grad_qkv, w_qkv_rel.T, preferred_element_type=F32)
    sums_rel = jnp.sum(grad_qkv.astype(F32), 0).reshape(peers, 3, cols)[:, :, : geo.real_cols]
    sums = jnp.stack([pick(list(sums_rel), own, g) for g in range(peers)], 1).reshape(3, D)
    grad_b_qv = jnp.concatenate([sums[0], sums[2]])
    grad_w_rel = jnp.einsum("td,te->de", normed_low, grad_qkv, preferred_element_type=F32)
    grad_w_rel = grad_w_rel.astype(BF16).reshape(D, peers, 3, cols)[..., : geo.real_cols]
    grad_w_qkv = jnp.stack(
        [pick([grad_w_rel[:, k] for k in range(peers)], own, g) for g in range(peers)], 2
    ).reshape(D, 3 * D)
    grad_inputs_norm, grad_ln1_gain, grad_ln1_bias = norm_first_back(grad_normed)
    grad_tokens = regroup(
        (grad_hidden + grad_inputs_norm).astype(BF16).reshape(wide, chunk, D)
    ).reshape(tokens.shape)

    def reduced(array):
        share = lax.psum_scatter(array.astype(BF16), "narrow", scatter_dimension=0, tiled=True)
        return lax.psum(share, "wide").astype(F32)

    narrow = lax.axis_size("narrow")
    vectors = [
        grad_b_qv,
        grad_b_out,
        grad_ls_attn,
        grad_ln1_gain,
        grad_ln1_bias,
        grad_ln2_gain,
        grad_ln2_bias,
        grad_b_fc1,
        grad_b_fc2,
        grad_ls_mlp,
    ]
    packed = jnp.concatenate([v.reshape(narrow, -1) for v in vectors], 1)
    packed = lax.psum_scatter(packed, "narrow", scatter_dimension=0, tiled=False)
    packed = lax.psum(packed, "wide")
    small, start = [], 0
    for v in vectors:
        size = v.shape[0] // narrow
        small.append(packed[start : start + size])
        start += size
    return (
        output,
        grad_tokens,
        reduced(grad_w_qkv),
        small[0],
        reduced(grad_w_out),
        small[1],
        small[2],
        small[3],
        small[4],
        small[5],
        small[6],
        reduced(grad_w_fc1),
        small[7],
        reduced(grad_w_fc2),
        small[8],
        small[9],
    )


def solution(mesh):
    rows = P("narrow", "wide", None, None, None)
    placed = (rows, P("narrow", "wide", None, None), rows) + (P(),) * 14
    matrix, vector = P("narrow", None), P("narrow")
    return jax.shard_map(
        per_device,
        mesh=mesh,
        in_specs=placed,
        out_specs=(
            rows,
            rows,
            matrix,
            vector,
            matrix,
            vector,
            vector,
            vector,
            vector,
            vector,
            vector,
            matrix,
            vector,
            matrix,
            vector,
            vector,
        ),
        check_vma=False,
    )
```

```python
import functools
import jax
import jax.numpy as jnp
from jax import lax
from jax.experimental import pallas as pl
from jax.experimental.pallas import tpu as pltpu
from jax.sharding import PartitionSpec as P

D = 768
HEADS = 12
HEAD = 64
GROUPS = 4
TILE = 512
KEYS = 512
LANES = 128
EPSILON = 1e-06
ROOT_HALF = 0.7071067811865476
FAR = -1e30
F32 = jnp.float32
BF16 = jnp.bfloat16


def layer_norm(values, gain, bias):
    average = jnp.mean(values, -1, keepdims=True)
    centred = values - average
    variance = jnp.mean(centred * centred, -1, keepdims=True)
    return centred * lax.rsqrt(variance + EPSILON) * gain + bias


def gelu_exact(values):
    return 0.5 * values * (1.0 + lax.erf(values * ROOT_HALF))


def dot_nt(a, b):
    return lax.dot_general(a, b, (((1,), (1,)), ((), ())), preferred_element_type=F32)


def dot_nn(a, b):
    return jnp.dot(a, b, preferred_element_type=F32)


class Geometry:
    def __init__(self, wide, piece):
        self.wide = wide
        self.piece = piece
        self.peers = wide // GROUPS
        self.chunk = piece // self.peers
        self.rows = wide * self.chunk
        self.slots = wide * piece
        heads = HEADS // self.peers
        self.real_cols = heads * HEAD
        self.pairs = (heads + 1) // 2
        self.cols = self.pairs * LANES
        self.tiles = self.slots // TILE


def gather_rows(geo, own, parts, column, fill):
    for back, part in enumerate(parts):
        source = lax.rem(own - back + geo.peers, geo.peers)
        for span in range(geo.wide):
            offset = pl.multiple_of(span * geo.piece + source * geo.chunk, geo.chunk)
            fill(offset, part[span, :, pl.ds(pl.multiple_of(column, LANES), LANES)])


def scatter_rows(geo, own, parts, column, source_ref):
    for back, part in enumerate(parts):
        source = lax.rem(own - back + geo.peers, geo.peers)
        for span in range(geo.wide):
            offset = pl.multiple_of(span * geo.piece + source * geo.chunk, geo.chunk)
            part[span, :, pl.ds(pl.multiple_of(column, LANES), LANES)] = source_ref[
                pl.ds(offset, geo.chunk), :
            ]


def attend_kernel(geo, table, *refs):
    peers = geo.peers
    qkv = refs[:peers]
    key_marks, query_marks = refs[peers : peers + 2]
    mixed = refs[peers + 2 : 2 * peers + 2]
    lse = refs[2 * peers + 2]
    ka, qa, va, ob, worst = refs[2 * peers + 3 :]
    pair = pl.program_id(0)
    own = table[0]
    first = lax.broadcasted_iota(jnp.int32, (geo.chunk, LANES), 1) < HEAD
    left = lax.broadcasted_iota(jnp.int32, (TILE, LANES), 1) < HEAD
    one = jnp.ones((geo.chunk, LANES), BF16)
    picks = lax.broadcasted_iota(jnp.int32, (8, LANES), 1) == HEAD * lax.broadcasted_iota(
        jnp.int32, (8, LANES), 0
    )

    def put_query(offset, values):
        marks = query_marks[pl.ds(offset, geo.chunk), :]
        scaled = values * 0.125
        qa[0, pl.ds(offset, geo.chunk), :] = jnp.where(first, scaled, marks)
        qa[1, pl.ds(offset, geo.chunk), :] = jnp.where(first, marks, scaled)

    def put_key(offset, values):
        marks = key_marks[pl.ds(offset, geo.chunk), :]
        ka[0, pl.ds(offset, geo.chunk), :] = jnp.where(first, values, marks)
        ka[1, pl.ds(offset, geo.chunk), :] = jnp.where(first, marks, values)

    def put_value(offset, values):
        va[0, pl.ds(offset, geo.chunk), :] = jnp.where(first, values, one)
        va[1, pl.ds(offset, geo.chunk), :] = jnp.where(first, one, values)

    gather_rows(geo, own, qkv, pair * LANES, put_query)
    gather_rows(geo, own, qkv, geo.cols + pair * LANES, put_key)
    gather_rows(geo, own, qkv, 2 * geo.cols + pair * LANES, put_value)

    def scores(which, step, at):
        return dot_nt(qa[which, pl.ds(at, TILE), :], ka[which, pl.ds(step, KEYS), :])

    def weighted(which, step, p):
        return dot_nn(p.astype(BF16), va[which, pl.ds(step, KEYS), :])

    def store(at, acc0, acc1, m0, m1):
        totals = pltpu.roll(jnp.where(left, acc1, acc0), HEAD, 1)
        ob[pl.ds(at, TILE), :] = (jnp.where(left, acc0, acc1) / totals).astype(BF16)
        logs = jnp.log(totals) + jnp.where(left, m0, m1)
        lse[0, :, pl.ds(at, TILE)] = lax.dot_general(
            picks.astype(F32),
            logs,
            (((1,), (1,)), ((), ())),
            precision=lax.Precision.HIGHEST,
            preferred_element_type=F32,
        )
        return totals

    def plain_tile(tile, _):
        at = pl.multiple_of(tile * TILE, TILE)

        def key_tile(index, carry):
            acc0, acc1 = carry
            step = pl.multiple_of(index * KEYS, KEYS)
            p0 = jnp.exp(scores(0, step, at))
            p1 = jnp.exp(scores(1, step, at))
            return acc0 + weighted(0, step, p0), acc1 + weighted(1, step, p1)

        blank = jnp.zeros((TILE, LANES), F32)
        acc0, acc1 = lax.fori_loop(
            table[1 + tile], table[1 + geo.tiles + tile], key_tile, (blank, blank)
        )
        totals = store(at, acc0, acc1, 0.0, 0.0)
        odd = jnp.where((totals > 1e-20) & (totals < 1e20), 0.0, 1.0)
        worst[...] = jnp.maximum(worst[...], jnp.max(odd.reshape(TILE // 8, 8, LANES), 0))
        return 0

    def careful_tile(tile, _):
        at = pl.multiple_of(tile * TILE, TILE)

        def one_head(which, step, m, acc):
            s = scores(which, step, at)
            m_new = jnp.maximum(m, jnp.max(s, 1, keepdims=True))
            acc = acc * jnp.exp(m - m_new) + weighted(which, step, jnp.exp(s - m_new))
            return m_new, acc

        def key_tile(index, carry):
            step = pl.multiple_of(index * KEYS, KEYS)
            return (*one_head(0, step, *carry[:2]), *one_head(1, step, *carry[2:]))

        low = jnp.full((TILE, 1), -2e30, F32)
        blank = jnp.zeros((TILE, LANES), F32)
        m0, acc0, m1, acc1 = lax.fori_loop(
            table[1 + tile], table[1 + geo.tiles + tile], key_tile, (low, blank, low, blank)
        )
        store(at, acc0, acc1, m0, m1)
        return 0

    worst[...] = jnp.zeros_like(worst)
    lax.fori_loop(0, geo.tiles, plain_tile, 0)

    @pl.when(jnp.max(worst[...]) > 0.0)
    def _():
        lax.fori_loop(0, geo.tiles, careful_tile, 0)

    scatter_rows(geo, own, mixed, pair * LANES, ob)


def attend_back_kernel(geo, table, *refs):
    peers = geo.peers
    qkv = refs[:peers]
    grads = refs[peers : 2 * peers]
    mixed = refs[2 * peers : 3 * peers]
    lse, key_marks, query_marks = refs[3 * peers : 3 * peers + 3]
    outs = refs[3 * peers + 3 : 4 * peers + 3]
    ka, qa, vn, qm, dm, kn, kt, dk, dv, ob, inner = refs[4 * peers + 3 :]
    pair = pl.program_id(0)
    own = table[0]
    lane = lax.broadcasted_iota(jnp.int32, (geo.chunk, LANES), 1)
    first = lane < HEAD
    zero = jnp.zeros((geo.chunk, LANES), BF16)
    half = lax.broadcasted_iota(jnp.int32, (8, LANES), 1) // HEAD == lax.broadcasted_iota(
        jnp.int32, (8, LANES), 0
    )
    half = half.astype(BF16)

    def put_query(offset, values):
        marks = query_marks[pl.ds(offset, geo.chunk), :]
        scaled = values * 0.125
        qa[0, pl.ds(offset, geo.chunk), :] = jnp.where(first, scaled, marks)
        qa[1, pl.ds(offset, geo.chunk), :] = jnp.where(first, marks, scaled)
        qm[0, pl.ds(offset, geo.chunk), :] = jnp.where(first, scaled, zero)
        qm[1, pl.ds(offset, geo.chunk), :] = jnp.where(first, zero, scaled)

    def put_key(offset, values):
        marks = key_marks[pl.ds(offset, geo.chunk), :]
        ka[0, pl.ds(offset, geo.chunk), :] = jnp.where(first, values, marks)
        ka[1, pl.ds(offset, geo.chunk), :] = jnp.where(first, marks, values)
        kn[pl.ds(offset, geo.chunk), :] = values

    def put_value(offset, values):
        vn[pl.ds(offset, geo.chunk), :] = values

    def put_mixed(offset, values):
        ob[pl.ds(offset, geo.chunk), :] = values

    def put_grad(offset, values):
        dm[0, pl.ds(offset, geo.chunk), :] = jnp.where(first, values, zero)
        dm[1, pl.ds(offset, geo.chunk), :] = jnp.where(first, zero, values)
        product = values.astype(F32) * ob[pl.ds(offset, geo.chunk), :].astype(F32)
        high = product.astype(BF16)
        rest = (product - high.astype(F32)).astype(BF16)
        kn[pl.ds(offset, geo.chunk), :] = high
        vn[pl.ds(offset, geo.chunk), :] = rest

    gather_rows(geo, own, mixed, pair * LANES, put_mixed)
    gather_rows(geo, own, grads, pair * LANES, put_grad)
    for tile in range(geo.tiles):
        rows = slice(tile * TILE, (tile + 1) * TILE)
        inner[:, rows] = dot_nt(half, kn[rows, :]) + dot_nt(half, vn[rows, :])
    gather_rows(geo, own, qkv, pair * LANES, put_query)
    gather_rows(geo, own, qkv, geo.cols + pair * LANES, put_key)
    gather_rows(geo, own, qkv, 2 * geo.cols + pair * LANES, put_value)
    for tile in range(geo.tiles):
        rows = slice(tile * TILE, (tile + 1) * TILE)
        kt[:, rows] = kn[rows, :].T
    dk[...] = jnp.zeros_like(dk)
    dv[...] = jnp.zeros_like(dv)

    def query_tile(tile, _):
        at = pl.multiple_of(tile * TILE, TILE)

        def one(which, step):
            s = dot_nt(ka[which, pl.ds(step, KEYS), :], qa[which, pl.ds(at, TILE), :])
            p = jnp.exp(s - lse[0, which : which + 1, pl.ds(at, TILE)])
            g = dot_nt(vn[pl.ds(step, KEYS), :], dm[which, pl.ds(at, TILE), :])
            ds = (p * (g - inner[which : which + 1, pl.ds(at, TILE)])).astype(BF16)
            return p.astype(BF16), ds

        def key_tile(index, carry):
            a0, a1 = carry
            step = pl.multiple_of(index * KEYS, KEYS)
            p0, s0 = one(0, step)
            p1, s1 = one(1, step)
            dv[pl.ds(step, KEYS), :] += dot_nn(p0, dm[0, pl.ds(at, TILE), :]) + dot_nn(
                p1, dm[1, pl.ds(at, TILE), :]
            )
            dk[pl.ds(step, KEYS), :] += dot_nn(s0, qm[0, pl.ds(at, TILE), :]) + dot_nn(
                s1, qm[1, pl.ds(at, TILE), :]
            )
            a0 = a0 + dot_nn(kt[:HEAD, pl.ds(step, KEYS)], s0)
            a1 = a1 + dot_nn(kt[HEAD:, pl.ds(step, KEYS)], s1)
            return a0, a1

        blank = jnp.zeros((HEAD, TILE), F32)
        a0, a1 = lax.fori_loop(
            table[1 + tile], table[1 + geo.tiles + tile], key_tile, (blank, blank)
        )
        ob[pl.ds(at, TILE), :] = (jnp.concatenate([a0, a1], 0) * 0.125).T.astype(BF16)
        return 0

    lax.fori_loop(0, geo.tiles, query_tile, 0)
    scatter_rows(geo, own, outs, pair * LANES, ob)
    ob[...] = dk[...].astype(BF16)
    scatter_rows(geo, own, outs, geo.cols + pair * LANES, ob)
    ob[...] = dv[...].astype(BF16)
    scatter_rows(geo, own, outs, 2 * geo.cols + pair * LANES, ob)


def whole_spec(shape):
    return pl.BlockSpec(shape, lambda pair, table: (0,) * len(shape))


def attend(geo, table, qkv_parts, key_marks, query_marks):
    out_shape = [
        jax.ShapeDtypeStruct((geo.wide, geo.chunk, geo.cols), BF16) for _ in range(geo.peers)
    ] + [jax.ShapeDtypeStruct((geo.pairs, 8, geo.slots), F32)]
    return pl.pallas_call(
        functools.partial(attend_kernel, geo),
        name="attend",
        out_shape=out_shape,
        grid_spec=pltpu.PrefetchScalarGridSpec(
            num_scalar_prefetch=1,
            grid=(geo.pairs,),
            in_specs=[whole_spec(a.shape) for a in qkv_parts]
            + [whole_spec((geo.slots, LANES))] * 2,
            out_specs=[whole_spec((geo.wide, geo.chunk, geo.cols))] * geo.peers
            + [pl.BlockSpec((1, 8, geo.slots), lambda pair, table: (pair, 0, 0))],
            scratch_shapes=[
                pltpu.VMEM((2, geo.slots, LANES), BF16),
                pltpu.VMEM((2, geo.slots, LANES), BF16),
                pltpu.VMEM((2, geo.slots, LANES), BF16),
                pltpu.VMEM((geo.slots, LANES), BF16),
                pltpu.VMEM((8, LANES), F32),
            ],
        ),
        cost_estimate=pl.CostEstimate(
            flops=4 * geo.slots * geo.slots * geo.real_cols,
            transcendentals=geo.slots * geo.slots * 6,
            bytes_accessed=4 * geo.slots * geo.cols * 2,
        ),
    )(table, *qkv_parts, key_marks, query_marks)


def attend_back(geo, table, qkv_parts, grad_parts, mixed_parts, lse, key_marks, query_marks):
    wide_shape = (geo.wide, geo.chunk, 3 * geo.cols)
    two = pltpu.VMEM((2, geo.slots, LANES), BF16)
    one = pltpu.VMEM((geo.slots, LANES), BF16)
    return pl.pallas_call(
        functools.partial(attend_back_kernel, geo),
        name="attend_back",
        out_shape=[jax.ShapeDtypeStruct(wide_shape, BF16) for _ in range(geo.peers)],
        grid_spec=pltpu.PrefetchScalarGridSpec(
            num_scalar_prefetch=1,
            grid=(geo.pairs,),
            in_specs=[whole_spec(a.shape) for a in (*qkv_parts, *grad_parts, *mixed_parts)]
            + [pl.BlockSpec((1, 8, geo.slots), lambda pair, table: (pair, 0, 0))]
            + [whole_spec((geo.slots, LANES))] * 2,
            out_specs=[whole_spec(wide_shape)] * geo.peers,
            scratch_shapes=[two, two, one, two, two, one]
            + [
                pltpu.VMEM((LANES, geo.slots), BF16),
                pltpu.VMEM((geo.slots, LANES), F32),
                pltpu.VMEM((geo.slots, LANES), F32),
                one,
                pltpu.VMEM((8, geo.slots), F32),
            ],
        ),
        cost_estimate=pl.CostEstimate(
            flops=10 * geo.slots * geo.slots * geo.real_cols,
            transcendentals=geo.slots * geo.slots * 6,
            bytes_accessed=12 * geo.slots * geo.cols * 2,
        ),
    )(table, *qkv_parts, *grad_parts, *mixed_parts, lse, key_marks, query_marks)


def flipped(place, k):
    bits = [place // 2**b % 2 for b in range(6)]
    return sum((1 - bit if k >> b & 1 else bit) * 2**b for b, bit in enumerate(bits))


def reduce_kernel(wide, peers, narrow, count, *refs):
    sources, outs = refs[:count], refs[count : 2 * count]
    firsts, partials, seconds, gathers = (
        refs[(2 + k) * count : (3 + k) * count] for k in range(4)
    )
    send_sems, recv_sems = refs[6 * count :]
    row = lax.axis_index("narrow")
    mine = lax.axis_index("wide")
    chip, peer = mine // peers, mine % peers

    barrier = pltpu.get_barrier_semaphore()
    for k in range(1, narrow):
        pl.semaphore_signal(
            barrier,
            inc=1,
            device_id={"narrow": flipped(row, k)},
            device_id_type=pl.DeviceIdType.MESH,
        )
    for k in range(1, wide):
        pl.semaphore_signal(
            barrier,
            inc=1,
            device_id={"wide": flipped(mine, k)},
            device_id_type=pl.DeviceIdType.MESH,
        )
    pl.semaphore_wait(barrier, narrow - 1 + wide - 1)

    def copy(job, index, source, target, device):
        return pltpu.make_async_remote_copy(
            src_ref=source,
            dst_ref=target,
            send_sem=send_sems.at[job, index],
            recv_sem=recv_sems.at[job, index],
            device_id=device,
            device_id_type=pl.DeviceIdType.MESH,
        )

    def to_row(job, k):
        target = flipped(row, k)
        return copy(
            job, k - 1, sources[job].at[target], firsts[job].at[k - 1], {"narrow": target}
        )

    def to_chip(job, k):
        target = flipped(chip, k)
        return copy(
            job,
            narrow - 2 + k,
            partials[job].at[target],
            seconds[job].at[k - 1],
            {"wide": target * peers + peer},
        )

    def spread(job, k):
        place = gathers[job].at[peer, chip]
        target = flipped(chip, k) * peers + peer
        return copy(job, narrow + GROUPS - 3 + k, place, place, {"wide": target})

    def to_peer(job, k, other):
        place = gathers[job].at[peer, flipped(chip, k)]
        index = narrow + 2 * GROUPS - 3 + k * (peers - 1) + other - 1
        return copy(job, index, place, place, {"wide": chip * peers + flipped(peer, other)})

    jobs = range(count)
    rows, chips, others = range(1, narrow), range(1, GROUPS), range(1, peers)
    started = [[to_row(job, k) for k in rows] for job in jobs]
    for copies in started:
        for c in copies:
            c.start()
    sent = [c for copies in started for c in copies]
    second = []
    for job in jobs:
        for c in started[job]:
            c.wait_recv()
        acc = sources[job][row].astype(F32)
        for k in rows:
            acc = acc + firsts[job][k - 1].astype(F32)
        partials[job][...] = acc.astype(partials[job].dtype)
        second.append([to_chip(job, k) for k in chips])
        for c in second[job]:
            c.start()
        sent += second[job]
    third, fourth = [], []
    for job in jobs:
        for c in second[job]:
            c.wait_recv()
        acc = partials[job][chip].astype(F32)
        for k in chips:
            acc = acc + seconds[job][k - 1].astype(F32)
        gathers[job][peer, chip] = acc.astype(gathers[job].dtype)
        third.append([spread(job, k) for k in chips])
        fourth.append([to_peer(job, 0, other) for other in others])
        for c in third[job] + fourth[job]:
            c.start()
    for job in jobs:
        for k in chips:
            third[job][k - 1].wait_recv()
            passed = [to_peer(job, k, other) for other in others]
            for c in passed:
                c.start()
            fourth[job] += passed
    for job in jobs:
        for c in fourth[job]:
            c.wait_recv()
        outs[job][...] = gathers[job][...]
        sent += third[job] + fourth[job]
    for c in sent:
        c.wait_send()


def reduce_everywhere(wide, peers, narrow, arrays):
    count = len(arrays)

    def scratch(*lead):
        return [pltpu.VMEM((*lead, *a.shape[2:]), a.dtype) for a in arrays]

    copies = narrow - 1 + 2 * (GROUPS - 1) + GROUPS * (peers - 1)
    in_vmem = pl.BlockSpec(memory_space=pltpu.VMEM)
    return pl.pallas_call(
        functools.partial(reduce_kernel, wide, peers, narrow, count),
        name="reduce_everywhere",
        out_shape=[jax.ShapeDtypeStruct((peers, *a.shape[1:]), a.dtype) for a in arrays],
        in_specs=[in_vmem] * count,
        out_specs=[in_vmem] * count,
        scratch_shapes=scratch(narrow - 1, GROUPS)
        + scratch(GROUPS)
        + scratch(GROUPS - 1)
        + scratch(peers, GROUPS)
        + [pltpu.SemaphoreType.DMA((count, copies)), pltpu.SemaphoreType.DMA((count, copies))],
        compiler_params=pltpu.CompilerParams(collective_id=1, has_side_effects=True),
        cost_estimate=pl.CostEstimate(
            flops=10**6, bytes_accessed=10**6, transcendentals=0
        ),
    )(*arrays)


def marks_of(block_ids, geo):
    lane = lax.broadcasted_iota(jnp.int32, (geo.slots, LANES), 1) % HEAD
    number = block_ids[:, None] + 1
    key_marks = (lane == number).astype(BF16)
    query_marks = jnp.where((lane < 9) & (lane != number), FAR, 0.0).astype(BF16)
    return key_marks, query_marks


def tile_table(block_ids, own, geo):
    def present(size):
        return jnp.any(block_ids.reshape(-1, size, 1) == jnp.arange(-1, 8, dtype=jnp.int32), 1)

    shared = jnp.any(present(TILE)[:, None] & present(KEYS)[None], -1)
    places = jnp.arange(geo.slots // KEYS, dtype=jnp.int32)
    low = jnp.min(jnp.where(shared, places, geo.tiles), 1)
    high = jnp.max(jnp.where(shared, places + 1, 0), 1)
    return jnp.concatenate([own[None], low, high]).astype(jnp.int32)


def pick(parts, own, target):
    peers = len(parts)
    result = parts[0]
    for step in range(1, peers):
        result = jnp.where((target - own + peers) % peers == step, parts[step], result)
    return result


def ahead(wide, peers, step):
    return [(w, w // peers * peers + (w % peers + step) % peers) for w in range(wide)]


def per_device(
    tokens,
    segment_ids,
    cotangent,
    w_qkv,
    b_qv,
    w_out,
    b_out,
    ls_attn,
    ln1_gain,
    ln1_bias,
    ln2_gain,
    ln2_bias,
    w_fc1,
    b_fc1,
    w_fc2,
    b_fc2,
    ls_mlp,
):
    geo = Geometry(lax.axis_size("wide"), tokens.shape[3])
    wide, peers, chunk, rows, cols = geo.wide, geo.peers, geo.chunk, geo.rows, geo.cols
    own = lax.axis_index("wide") % peers

    def regroup(array):
        return lax.all_to_all(array, "wide", split_axis=0, concat_axis=0, tiled=True)

    token_rows = regroup(tokens.reshape(wide, chunk, D)).reshape(rows, D)
    cotangent, segment_ids, token_rows = lax.optimization_barrier(
        (cotangent, segment_ids, token_rows)
    )
    ids_out = jnp.broadcast_to(segment_ids.reshape(GROUPS, 1, geo.piece), (GROUPS, peers, geo.piece))
    block_ids = regroup(ids_out.reshape(wide, geo.piece)).reshape(geo.slots)
    cotangent_rows = regroup(cotangent.reshape(wide, chunk, D)).reshape(rows, D)

    my_ids = lax.dynamic_index_in_dim(
        block_ids.reshape(wide, peers, chunk), own, 1, keepdims=False
    ).reshape(rows, 1)
    valid_rows = (my_ids >= 0).astype(F32)
    key_marks, query_marks = marks_of(block_ids, geo)
    table = tile_table(block_ids, own, geo)

    bias_all = jnp.concatenate([b_qv[:D], jnp.zeros((D,), F32), b_qv[D:]])
    w_heads = w_qkv.reshape(D, 3, peers, geo.real_cols)
    b_heads = bias_all.reshape(3, peers, geo.real_cols)
    o_heads = w_out.reshape(peers, geo.real_cols, D)
    spare = cols - geo.real_cols

    w_own = lax.dynamic_index_in_dim(w_heads, own, 2, keepdims=False)
    w_own = jnp.pad(w_own, ((0, 0), (0, 0), (0, spare))).reshape(D, 3 * cols)
    b_own = lax.dynamic_index_in_dim(b_heads, own, 1, keepdims=False)
    b_own = jnp.pad(b_own, ((0, 0), (0, spare))).reshape(3 * cols)

    def outward_of(step):
        o = lax.dynamic_index_in_dim(o_heads, (own + step) % peers, 0, keepdims=False)
        return jnp.pad(o, ((0, spare), (0, 0)))

    o_parts = [outward_of(step) for step in range(peers)]

    def send(array, step):
        return lax.ppermute(array, "wide", ahead(wide, peers, step % peers))

    def peer_share(left, right):
        width = right.shape[1] // peers

        def product(step):
            start = (own + step) % peers * width
            some = lax.dynamic_slice_in_dim(right, start, width, 1)
            return lax.dot_general(left, some, (((0,), (0,)), ((), ())), preferred_element_type=F32)

        travels = [send(product(step).astype(BF16), step) for step in range(1, peers)]
        return (product(0) + sum(t.astype(F32) for t in travels)).astype(BF16)

    def scattered(array):
        return lax.psum_scatter(array, "narrow", scatter_dimension=0, tiled=True)

    def over_chips(array):
        return lax.psum(array, "wide", axis_index_groups=[
            list(range(p, wide, peers)) for p in range(peers)
        ])

    def swap_chips(array, k):
        pairs = [(w, (w // peers ^ k) * peers + w % peers) for w in range(wide)]
        return lax.ppermute(array, "wide", pairs)

    def paired(place, mine, theirs, axis):
        low, high = jnp.where(place == 0, mine, theirs), jnp.where(place == 0, theirs, mine)
        return jnp.stack([low, high], axis)

    def in_order(parts, place):
        bit = 1
        while bit < len(parts):
            odd = place // bit % 2 == 1
            parts = [jnp.where(odd, parts[k ^ bit], parts[k]) for k in range(len(parts))]
            bit *= 2
        return parts

    def added(a, b):
        return (a.astype(F32) + b.astype(F32)).astype(BF16)

    def held(*values):
        return lax.optimization_barrier(values)

    def over_peers(array):
        return lax.all_gather(array, "wide", axis_index_groups=[
            list(range(g, g + peers)) for g in range(0, wide, peers)
        ])

    inputs = token_rows.astype(F32)
    normed, norm_first_back = jax.vjp(layer_norm, inputs, ln1_gain, ln1_bias)
    normed_low = normed.astype(BF16)
    normed_parts = [normed_low] + [send(normed_low, step) for step in range(1, peers)]
    qkv_parts = [
        (dot_nn(part, w_own) + b_own).astype(BF16).reshape(wide, chunk, 3 * cols)
        for part in normed_parts
    ]
    *mixed_parts, lse = attend(geo, table, qkv_parts, key_marks, query_marks)
    mixed_parts, cotangent_rows = lax.optimization_barrier((mixed_parts, cotangent_rows))
    mixed_home = [
        (send(part, -step) if step else part).reshape(rows, cols)
        for step, part in enumerate(mixed_parts)
    ]
    mixed_rows = jnp.concatenate(mixed_home, 1)
    w_out_rel = jnp.concatenate(o_parts, 0)
    projected = dot_nn(mixed_rows, w_out_rel) + b_out
    hidden = inputs + ls_attn * projected
    second, norm_second_back = jax.vjp(layer_norm, hidden, ln2_gain, ln2_bias)
    second_low = second.astype(BF16)
    pre_act = dot_nn(second_low, w_fc1) + b_fc1
    activation, gelu_back = jax.vjp(gelu_exact, pre_act)
    act_low = activation.astype(BF16)
    mlp_out = dot_nn(act_low, w_fc2) + b_fc2
    result = ((hidden + ls_mlp * mlp_out) * valid_rows).astype(BF16)
    output = regroup(result.reshape(wide, chunk, D)).reshape(tokens.shape)
    grad_out = cotangent_rows.astype(F32) * valid_rows
    grad_ls_mlp = jnp.sum(grad_out * mlp_out, 0)
    grad_mlp = (ls_mlp * grad_out).astype(BF16)
    grad_b_fc2 = jnp.sum(grad_mlp.astype(F32), 0)
    grad_w_fc2 = peer_share(act_low, grad_mlp)
    grad_act = jnp.dot(grad_mlp, w_fc2.T, preferred_element_type=F32)
    grad_pre = gelu_back(grad_act)[0].astype(BF16)
    grad_pre, grad_w_fc2 = lax.optimization_barrier((grad_pre, grad_w_fc2))
    sums_fc2 = scattered(grad_w_fc2)
    grad_b_fc1 = jnp.sum(grad_pre.astype(F32), 0)
    grad_w_fc1 = peer_share(second_low, grad_pre)
    grad_second = jnp.dot(grad_pre, w_fc1.T, preferred_element_type=F32)
    grad_hidden_norm, grad_ln2_gain, grad_ln2_bias = norm_second_back(grad_second)
    grad_hidden = grad_out + grad_hidden_norm
    grad_ls_attn = jnp.sum(grad_hidden * projected, 0)
    grad_proj = (ls_attn * grad_hidden).astype(BF16)
    grad_b_out = jnp.sum(grad_proj.astype(F32), 0)
    proj_parts = [grad_proj] + [send(grad_proj, step) for step in range(1, peers)]
    mixed_plain = jnp.concatenate(
        [pick([m[:, : geo.real_cols] for m in mixed_home], own, g) for g in range(peers)], 1
    )
    grad_w_out = peer_share(mixed_plain, grad_proj)
    grad_parts = [
        jnp.dot(part, o_parts[0].T, preferred_element_type=F32)
        .astype(BF16)
        .reshape(wide, chunk, cols)
        for part in proj_parts
    ]
    narrow = lax.axis_size("narrow")
    wide_half = grad_w_fc1.shape[1]
    grad_w_both = jnp.concatenate(
        [
            grad_w_fc1.reshape(narrow, -1, wide_half),
            grad_w_out.reshape(narrow, -1, wide_half),
        ],
        1,
    ).reshape(-1, wide_half)
    grad_parts, grad_w_both, sums_fc2, output = lax.optimization_barrier(
        (grad_parts, grad_w_both, sums_fc2, output)
    )
    sums_both = scattered(grad_w_both)

    dqkv_parts = attend_back(
        geo, table, qkv_parts, grad_parts, mixed_parts, lse, key_marks, query_marks
    )
    share, step_width = D // narrow, D // peers
    chip = lax.axis_index("wide") // peers
    near, far = chip % 2, chip // 2
    quarters = jnp.stack(
        [sums_both[:, k * step_width : (k + 1) * step_width] for k in range(GROUPS)]
    )
    quarters = jnp.concatenate([sums_fc2.reshape(GROUPS, share, step_width), quarters], 1)
    quarters, dqkv_parts = held(quarters, dqkv_parts)
    quarters = quarters.reshape(2, 2, -1, step_width)
    going = lax.dynamic_index_in_dim(quarters, 1 - near, 1, keepdims=False)
    staying = lax.dynamic_index_in_dim(quarters, near, 1, keepdims=False)
    going, staying, dqkv_parts = held(going, staying, dqkv_parts)
    came = swap_chips(going, 1)
    dqkv_parts = [part.reshape(rows, 3 * cols) for part in dqkv_parts]
    partial = [
        jnp.dot(part, w_own.T, preferred_element_type=F32) for part in dqkv_parts
    ]
    for step in range(1, peers):
        partial[step] = send(partial[step].astype(BF16), -step)
    partial, came = held(partial, came)
    halves = added(staying, came)
    going = lax.dynamic_index_in_dim(halves, 1 - far, 0, keepdims=False)
    staying = lax.dynamic_index_in_dim(halves, far, 0, keepdims=False)
    going, staying, partial = held(going, staying, partial)
    came = swap_chips(going, 2)
    grad_normed = partial[0]
    for step in range(1, peers):
        grad_normed = grad_normed + partial[step].astype(F32)
    grad_w_qkv = sum(
        jnp.einsum("td,te->de", a, b, preferred_element_type=F32)
        for a, b in zip(normed_parts, dqkv_parts)
    ).astype(BF16)
    sums = sum(jnp.sum(part.astype(F32), 0) for part in dqkv_parts)
    sums = sums.reshape(3, 1, cols)[:, :, : geo.real_cols]
    sums = jnp.where(jnp.arange(peers)[:, None] == own, sums, 0.0)
    grad_b_qv = sums[::2].reshape(2 * D)
    grad_inputs_norm, grad_ln1_gain, grad_ln1_bias = norm_first_back(grad_normed)
    grad_rows = (grad_hidden + grad_inputs_norm).astype(BF16)
    came, _ = held(came, grad_rows)
    quarter = added(staying, came)
    quarter, grad_w_qkv = held(quarter, grad_w_qkv)
    came = swap_chips(quarter, 2)
    grad_tokens = regroup(grad_rows.reshape(wide, chunk, D)).reshape(tokens.shape)

    vectors = [
        grad_b_qv,
        grad_b_out,
        grad_ls_attn,
        grad_ln1_gain,
        grad_ln1_bias,
        grad_ln2_gain,
        grad_ln2_bias,
        grad_b_fc1,
        grad_b_fc2,
        grad_ls_mlp,
    ]
    flat = jnp.concatenate([v.reshape(narrow, -1) for v in vectors], 1)
    flat = jnp.pad(flat, ((0, 0), (0, -flat.shape[1] % (GROUPS * 8 * LANES))))
    flat = flat.reshape(narrow, GROUPS, -1, LANES)
    thirds = [
        grad_w_qkv[:, t * cols : (t + 1) * cols].reshape(narrow, GROUPS, -1, cols)
        for t in range(3)
    ]
    came, flat, thirds = held(came, flat, thirds)
    pair = paired(far, quarter, came, 0)
    pair, flat, thirds = held(pair, flat, thirds)
    came = swap_chips(pair, 1)
    if narrow <= GROUPS:
        flat, *thirds = reduce_everywhere(wide, peers, narrow, [flat, *thirds])
    else:
        flat, *thirds = (
            over_peers(over_chips(scattered(a))).reshape(peers, *a.shape[1:])
            for a in (flat, *thirds)
        )

    came, flat, thirds = held(came, flat, thirds)
    whole_share = paired(near, pair, came, 1).reshape(GROUPS, -1, step_width)
    parts = [whole_share]
    for k in range(1, peers):
        parts.append(lax.ppermute(whole_share, "wide", [(w, w ^ k) for w in range(wide)]))
    everything = jnp.stack(in_order(parts, own))
    flat = sum(flat[p] for p in range(peers)).reshape(-1)
    small, start = [], 0
    for v in vectors:
        size = v.shape[0] // narrow
        small.append(flat[start : start + size])
        start += size
    sums_fc2 = everything[:, :, :share].reshape(peers, GROUPS * share, step_width)
    sums_both = jnp.concatenate([everything[:, k, share:] for k in range(GROUPS)], 2)
    sums_out = sums_both[:, share:].reshape(peers, share, step_width)
    done_qkv = jnp.concatenate(
        [
            third[p].reshape(share, cols)[:, : geo.real_cols]
            for third in thirds
            for p in range(peers)
        ],
        1,
    ).astype(F32)

    def side_by_side(array):
        return array.transpose(1, 0, 2).reshape(array.shape[1], -1).astype(F32)

    return (
        output,
        grad_tokens,
        done_qkv,
        small[0],
        side_by_side(sums_out),
        small[1],
        small[2],
        small[3],
        small[4],
        small[5],
        small[6],
        side_by_side(sums_both[:, :share]),
        small[7],
        side_by_side(sums_fc2),
        small[8],
        small[9],
    )


def solution(mesh):
    rows = P("narrow", "wide", None, None, None)
    placed = (rows, P("narrow", "wide", None, None), rows) + (P(),) * 14
    matrix, vector = P("narrow", None), P("narrow")
    return jax.shard_map(
        per_device,
        mesh=mesh,
        in_specs=placed,
        out_specs=(
            rows,
            rows,
            matrix,
            vector,
            matrix,
            vector,
            vector,
            vector,
            vector,
            vector,
            vector,
            matrix,
            vector,
            matrix,
            vector,
            vector,
        ),
        check_vma=False,
    )
```

```python
import functools
import jax
import jax.numpy as jnp
from jax import lax
from jax.experimental import pallas as pl
from jax.experimental.pallas import tpu as pltpu
from jax.sharding import PartitionSpec as P

D = 768
HEADS = 12
HEAD = 64
GROUPS = 4
TILE = 512
KEYS = 512
LANES = 128
EPSILON = 1e-06
ROOT_HALF = 0.7071067811865476
FAR = -1e30
F32 = jnp.float32
BF16 = jnp.bfloat16


def layer_norm(values, gain, bias):
    average = jnp.mean(values, -1, keepdims=True)
    centred = values - average
    variance = jnp.mean(centred * centred, -1, keepdims=True)
    return centred * lax.rsqrt(variance + EPSILON) * gain + bias


def gelu_exact(values):
    return 0.5 * values * (1.0 + lax.erf(values * ROOT_HALF))


def dot_nt(a, b):
    return lax.dot_general(a, b, (((1,), (1,)), ((), ())), preferred_element_type=F32)


def dot_nn(a, b):
    return jnp.dot(a, b, preferred_element_type=F32)


class Geometry:
    def __init__(self, wide, piece):
        self.wide = wide
        self.piece = piece
        self.peers = wide // GROUPS
        self.chunk = piece // self.peers
        self.rows = wide * self.chunk
        self.slots = wide * piece
        heads = HEADS // self.peers
        self.real_cols = heads * HEAD
        self.pairs = (heads + 1) // 2
        self.cols = self.pairs * LANES
        self.tiles = self.slots // TILE


def gather_rows(geo, own, parts, column, fill):
    for back, part in enumerate(parts):
        source = lax.rem(own - back + geo.peers, geo.peers)
        for span in range(geo.wide):
            offset = pl.multiple_of(span * geo.piece + source * geo.chunk, geo.chunk)
            fill(offset, part[span, :, pl.ds(pl.multiple_of(column, LANES), LANES)])


def scatter_rows(geo, own, parts, column, source_ref):
    for back, part in enumerate(parts):
        source = lax.rem(own - back + geo.peers, geo.peers)
        for span in range(geo.wide):
            offset = pl.multiple_of(span * geo.piece + source * geo.chunk, geo.chunk)
            part[span, :, pl.ds(pl.multiple_of(column, LANES), LANES)] = source_ref[
                pl.ds(offset, geo.chunk), :
            ]


def attend_kernel(geo, table, *refs):
    peers = geo.peers
    qkv = refs[:peers]
    key_marks, query_marks = refs[peers : peers + 2]
    mixed = refs[peers + 2 : 2 * peers + 2]
    lse = refs[2 * peers + 2]
    ka, qa, va, ob, worst = refs[2 * peers + 3 :]
    pair = pl.program_id(0)
    own = table[0]
    first = lax.broadcasted_iota(jnp.int32, (geo.chunk, LANES), 1) < HEAD
    left = lax.broadcasted_iota(jnp.int32, (TILE, LANES), 1) < HEAD
    one = jnp.ones((geo.chunk, LANES), BF16)
    picks = lax.broadcasted_iota(jnp.int32, (8, LANES), 1) == HEAD * lax.broadcasted_iota(
        jnp.int32, (8, LANES), 0
    )

    def put_query(offset, values):
        marks = query_marks[pl.ds(offset, geo.chunk), :]
        scaled = values * 0.125
        qa[0, pl.ds(offset, geo.chunk), :] = jnp.where(first, scaled, marks)
        qa[1, pl.ds(offset, geo.chunk), :] = jnp.where(first, marks, scaled)

    def put_key(offset, values):
        marks = key_marks[pl.ds(offset, geo.chunk), :]
        ka[0, pl.ds(offset, geo.chunk), :] = jnp.where(first, values, marks)
        ka[1, pl.ds(offset, geo.chunk), :] = jnp.where(first, marks, values)

    def put_value(offset, values):
        va[0, pl.ds(offset, geo.chunk), :] = jnp.where(first, values, one)
        va[1, pl.ds(offset, geo.chunk), :] = jnp.where(first, one, values)

    gather_rows(geo, own, qkv, pair * LANES, put_query)
    gather_rows(geo, own, qkv, geo.cols + pair * LANES, put_key)
    gather_rows(geo, own, qkv, 2 * geo.cols + pair * LANES, put_value)

    def scores(which, step, at):
        return dot_nt(qa[which, pl.ds(at, TILE), :], ka[which, pl.ds(step, KEYS), :])

    def weighted(which, step, p):
        return dot_nn(p.astype(BF16), va[which, pl.ds(step, KEYS), :])

    def store(at, acc0, acc1, m0, m1):
        totals = pltpu.roll(jnp.where(left, acc1, acc0), HEAD, 1)
        ob[pl.ds(at, TILE), :] = (jnp.where(left, acc0, acc1) / totals).astype(BF16)
        logs = jnp.log(totals) + jnp.where(left, m0, m1)
        lse[0, :, pl.ds(at, TILE)] = lax.dot_general(
            picks.astype(F32),
            logs,
            (((1,), (1,)), ((), ())),
            precision=lax.Precision.HIGHEST,
            preferred_element_type=F32,
        )
        return totals

    def plain_tile(tile, _):
        at = pl.multiple_of(tile * TILE, TILE)

        def key_tile(index, carry):
            acc0, acc1 = carry
            step = pl.multiple_of(index * KEYS, KEYS)
            p0 = jnp.exp(scores(0, step, at))
            p1 = jnp.exp(scores(1, step, at))
            return acc0 + weighted(0, step, p0), acc1 + weighted(1, step, p1)

        blank = jnp.zeros((TILE, LANES), F32)
        acc0, acc1 = lax.fori_loop(
            table[1 + tile], table[1 + geo.tiles + tile], key_tile, (blank, blank)
        )
        totals = store(at, acc0, acc1, 0.0, 0.0)
        odd = jnp.where((totals > 1e-20) & (totals < 1e20), 0.0, 1.0)
        worst[...] = jnp.maximum(worst[...], jnp.max(odd.reshape(TILE // 8, 8, LANES), 0))
        return 0

    def careful_tile(tile, _):
        at = pl.multiple_of(tile * TILE, TILE)

        def one_head(which, step, m, acc):
            s = scores(which, step, at)
            m_new = jnp.maximum(m, jnp.max(s, 1, keepdims=True))
            acc = acc * jnp.exp(m - m_new) + weighted(which, step, jnp.exp(s - m_new))
            return m_new, acc

        def key_tile(index, carry):
            step = pl.multiple_of(index * KEYS, KEYS)
            return (*one_head(0, step, *carry[:2]), *one_head(1, step, *carry[2:]))

        low = jnp.full((TILE, 1), -2e30, F32)
        blank = jnp.zeros((TILE, LANES), F32)
        m0, acc0, m1, acc1 = lax.fori_loop(
            table[1 + tile], table[1 + geo.tiles + tile], key_tile, (low, blank, low, blank)
        )
        store(at, acc0, acc1, m0, m1)
        return 0

    worst[...] = jnp.zeros_like(worst)
    lax.fori_loop(0, geo.tiles, plain_tile, 0)

    @pl.when(jnp.max(worst[...]) > 0.0)
    def _():
        lax.fori_loop(0, geo.tiles, careful_tile, 0)

    scatter_rows(geo, own, mixed, pair * LANES, ob)


def attend_back_kernel(geo, begin, count, table, *refs):
    peers = geo.peers
    qkv = refs[:peers]
    grads = refs[peers : 2 * peers]
    mixed = refs[2 * peers : 3 * peers]
    lse, key_marks, query_marks = refs[3 * peers : 3 * peers + 3]
    outs = refs[3 * peers + 3 : 4 * peers + 3]
    ka, qa, vn, qm, dm, kn, kt, dk, dv, ob, inner = refs[4 * peers + 3 :]
    step_pair = pl.program_id(0)
    pair = begin + step_pair
    own = table[0]
    lane = lax.broadcasted_iota(jnp.int32, (geo.chunk, LANES), 1)
    first = lane < HEAD
    zero = jnp.zeros((geo.chunk, LANES), BF16)
    half = lax.broadcasted_iota(jnp.int32, (8, LANES), 1) // HEAD == lax.broadcasted_iota(
        jnp.int32, (8, LANES), 0
    )
    half = half.astype(BF16)

    def put_query(offset, values):
        marks = query_marks[pl.ds(offset, geo.chunk), :]
        scaled = values * 0.125
        qa[0, pl.ds(offset, geo.chunk), :] = jnp.where(first, scaled, marks)
        qa[1, pl.ds(offset, geo.chunk), :] = jnp.where(first, marks, scaled)
        qm[0, pl.ds(offset, geo.chunk), :] = jnp.where(first, scaled, zero)
        qm[1, pl.ds(offset, geo.chunk), :] = jnp.where(first, zero, scaled)

    def put_key(offset, values):
        marks = key_marks[pl.ds(offset, geo.chunk), :]
        ka[0, pl.ds(offset, geo.chunk), :] = jnp.where(first, values, marks)
        ka[1, pl.ds(offset, geo.chunk), :] = jnp.where(first, marks, values)
        kn[pl.ds(offset, geo.chunk), :] = values

    def put_value(offset, values):
        vn[pl.ds(offset, geo.chunk), :] = values

    def put_mixed(offset, values):
        ob[pl.ds(offset, geo.chunk), :] = values

    def put_grad(offset, values):
        dm[0, pl.ds(offset, geo.chunk), :] = jnp.where(first, values, zero)
        dm[1, pl.ds(offset, geo.chunk), :] = jnp.where(first, zero, values)
        product = values.astype(F32) * ob[pl.ds(offset, geo.chunk), :].astype(F32)
        high = product.astype(BF16)
        rest = (product - high.astype(F32)).astype(BF16)
        kn[pl.ds(offset, geo.chunk), :] = high
        vn[pl.ds(offset, geo.chunk), :] = rest

    gather_rows(geo, own, mixed, pair * LANES, put_mixed)
    gather_rows(geo, own, grads, pair * LANES, put_grad)
    for tile in range(geo.tiles):
        rows = slice(tile * TILE, (tile + 1) * TILE)
        inner[:, rows] = dot_nt(half, kn[rows, :]) + dot_nt(half, vn[rows, :])
    gather_rows(geo, own, qkv, pair * LANES, put_query)
    gather_rows(geo, own, qkv, geo.cols + pair * LANES, put_key)
    gather_rows(geo, own, qkv, 2 * geo.cols + pair * LANES, put_value)
    for tile in range(geo.tiles):
        rows = slice(tile * TILE, (tile + 1) * TILE)
        kt[:, rows] = kn[rows, :].T
    dk[...] = jnp.zeros_like(dk)
    dv[...] = jnp.zeros_like(dv)

    def query_tile(tile, _):
        at = pl.multiple_of(tile * TILE, TILE)

        def one(which, step):
            s = dot_nt(ka[which, pl.ds(step, KEYS), :], qa[which, pl.ds(at, TILE), :])
            p = jnp.exp(s - lse[0, which : which + 1, pl.ds(at, TILE)])
            g = dot_nt(vn[pl.ds(step, KEYS), :], dm[which, pl.ds(at, TILE), :])
            ds = (p * (g - inner[which : which + 1, pl.ds(at, TILE)])).astype(BF16)
            return p.astype(BF16), ds

        def key_tile(index, carry):
            a0, a1 = carry
            step = pl.multiple_of(index * KEYS, KEYS)
            p0, s0 = one(0, step)
            p1, s1 = one(1, step)
            dv[pl.ds(step, KEYS), :] += dot_nn(p0, dm[0, pl.ds(at, TILE), :]) + dot_nn(
                p1, dm[1, pl.ds(at, TILE), :]
            )
            dk[pl.ds(step, KEYS), :] += dot_nn(s0, qm[0, pl.ds(at, TILE), :]) + dot_nn(
                s1, qm[1, pl.ds(at, TILE), :]
            )
            a0 = a0 + dot_nn(kt[:HEAD, pl.ds(step, KEYS)], s0)
            a1 = a1 + dot_nn(kt[HEAD:, pl.ds(step, KEYS)], s1)
            return a0, a1

        blank = jnp.zeros((HEAD, TILE), F32)
        a0, a1 = lax.fori_loop(
            table[1 + tile], table[1 + geo.tiles + tile], key_tile, (blank, blank)
        )
        ob[pl.ds(at, TILE), :] = (jnp.concatenate([a0, a1], 0) * 0.125).T.astype(BF16)
        return 0

    lax.fori_loop(0, geo.tiles, query_tile, 0)
    scatter_rows(geo, own, outs, step_pair * LANES, ob)
    ob[...] = dk[...].astype(BF16)
    scatter_rows(geo, own, outs, (count + step_pair) * LANES, ob)
    ob[...] = dv[...].astype(BF16)
    scatter_rows(geo, own, outs, (2 * count + step_pair) * LANES, ob)


def whole_spec(shape):
    return pl.BlockSpec(shape, lambda pair, table: (0,) * len(shape))


def attend(geo, table, qkv_parts, key_marks, query_marks):
    out_shape = [
        jax.ShapeDtypeStruct((geo.wide, geo.chunk, geo.cols), BF16) for _ in range(geo.peers)
    ] + [jax.ShapeDtypeStruct((geo.pairs, 8, geo.slots), F32)]
    return pl.pallas_call(
        functools.partial(attend_kernel, geo),
        name="attend",
        out_shape=out_shape,
        grid_spec=pltpu.PrefetchScalarGridSpec(
            num_scalar_prefetch=1,
            grid=(geo.pairs,),
            in_specs=[whole_spec(a.shape) for a in qkv_parts]
            + [whole_spec((geo.slots, LANES))] * 2,
            out_specs=[whole_spec((geo.wide, geo.chunk, geo.cols))] * geo.peers
            + [pl.BlockSpec((1, 8, geo.slots), lambda pair, table: (pair, 0, 0))],
            scratch_shapes=[
                pltpu.VMEM((2, geo.slots, LANES), BF16),
                pltpu.VMEM((2, geo.slots, LANES), BF16),
                pltpu.VMEM((2, geo.slots, LANES), BF16),
                pltpu.VMEM((geo.slots, LANES), BF16),
                pltpu.VMEM((8, LANES), F32),
            ],
        ),
        cost_estimate=pl.CostEstimate(
            flops=4 * geo.slots * geo.slots * geo.real_cols,
            transcendentals=geo.slots * geo.slots * 6,
            bytes_accessed=4 * geo.slots * geo.cols * 2,
        ),
    )(table, *qkv_parts, key_marks, query_marks)


def attend_back(geo, begin, count, table, qkv_parts, grad_parts, mixed_parts, lse, key_marks, query_marks):
    wide_shape = (geo.wide, geo.chunk, 3 * count * LANES)
    two = pltpu.VMEM((2, geo.slots, LANES), BF16)
    one = pltpu.VMEM((geo.slots, LANES), BF16)
    return pl.pallas_call(
        functools.partial(attend_back_kernel, geo, begin, count),
        name=f"attend_back_{begin}",
        out_shape=[jax.ShapeDtypeStruct(wide_shape, BF16) for _ in range(geo.peers)],
        grid_spec=pltpu.PrefetchScalarGridSpec(
            num_scalar_prefetch=1,
            grid=(count,),
            in_specs=[whole_spec(a.shape) for a in (*qkv_parts, *grad_parts, *mixed_parts)]
            + [pl.BlockSpec((1, 8, geo.slots), lambda pair, table: (begin + pair, 0, 0))]
            + [whole_spec((geo.slots, LANES))] * 2,
            out_specs=[whole_spec(wide_shape)] * geo.peers,
            scratch_shapes=[two, two, one, two, two, one]
            + [
                pltpu.VMEM((LANES, geo.slots), BF16),
                pltpu.VMEM((geo.slots, LANES), F32),
                pltpu.VMEM((geo.slots, LANES), F32),
                one,
                pltpu.VMEM((8, geo.slots), F32),
            ],
        ),
        cost_estimate=pl.CostEstimate(
            flops=10 * geo.slots * geo.slots * count * LANES,
            transcendentals=geo.slots * geo.slots * 2 * count,
            bytes_accessed=12 * geo.slots * geo.cols * 2,
        ),
    )(table, *qkv_parts, *grad_parts, *mixed_parts, lse, key_marks, query_marks)


def flipped(place, k):
    bits = [place // 2**b % 2 for b in range(6)]
    return sum((1 - bit if k >> b & 1 else bit) * 2**b for b, bit in enumerate(bits))


def reduce_kernel(wide, peers, narrow, count, *refs):
    sources, given = refs[:count], refs[count]
    outs = refs[count + 1 : 2 * count + 2]
    scratch = refs[2 * count + 2 :]
    firsts, partials, seconds = (scratch[k * count : (k + 1) * count] for k in range(3))
    gathers = scratch[3 * count : 4 * count + 1]
    send_sems, recv_sems = scratch[4 * count + 1 :]
    row = lax.axis_index("narrow")
    mine = lax.axis_index("wide")
    chip, peer = mine // peers, mine % peers

    barrier = pltpu.get_barrier_semaphore()
    for k in range(1, narrow):
        pl.semaphore_signal(
            barrier,
            inc=1,
            device_id={"narrow": flipped(row, k)},
            device_id_type=pl.DeviceIdType.MESH,
        )
    for k in range(1, wide):
        pl.semaphore_signal(
            barrier,
            inc=1,
            device_id={"wide": flipped(mine, k)},
            device_id_type=pl.DeviceIdType.MESH,
        )
    pl.semaphore_wait(barrier, narrow - 1 + wide - 1)

    def copy(job, index, source, target, device):
        return pltpu.make_async_remote_copy(
            src_ref=source,
            dst_ref=target,
            send_sem=send_sems.at[job, index],
            recv_sem=recv_sems.at[job, index],
            device_id=device,
            device_id_type=pl.DeviceIdType.MESH,
        )

    def to_row(job, k):
        target = flipped(row, k)
        return copy(
            job, k - 1, sources[job].at[target], firsts[job].at[k - 1], {"narrow": target}
        )

    def to_chip(job, k):
        target = flipped(chip, k)
        return copy(
            job,
            narrow - 2 + k,
            partials[job].at[target],
            seconds[job].at[k - 1],
            {"wide": target * peers + peer},
        )

    rows, chips, others = range(1, narrow), range(1, GROUPS), range(1, peers)
    after_chips = narrow + GROUPS - 2
    near, far = flipped(chip, 1), flipped(chip, 2)

    def place(job, k):
        return gathers[job].at[peer, flipped(chip, k)]

    def own(job):
        return given if job == count else place(job, 0)

    def to_far(job):
        return copy(job, after_chips, own(job), place(job, 0), {"wide": far * peers + peer})

    def to_near(job):
        return copy(job, after_chips + 1, own(job), place(job, 0), {"wide": near * peers + peer})

    def relay(job):
        target = {"wide": near * peers + peer}
        return copy(job, after_chips + 2, place(job, 2), place(job, 2), target)

    sent, passed = [], [[] for _ in gathers]

    def go(copies):
        for c in copies:
            c.start()
        sent.extend(copies)
        return copies

    def to_peers(job, k):
        source = place(job, k) if k else own(job)
        passed[job] += go(
            [
                copy(
                    job,
                    after_chips + 3 + k * (peers - 1) + other - 1,
                    source,
                    place(job, k),
                    {"wide": chip * peers + flipped(peer, other)},
                )
                for other in others
            ]
        )

    jobs = range(count)
    offers = {}

    def offer(job):
        offers[job] = go([to_far(job), to_near(job)])
        to_peers(job, 0)

    def from_far(job):
        offers[job][0].wait_recv()
        offers[job] += go([relay(job)])
        to_peers(job, 2)

    def from_near(job):
        offers[job][1].wait_recv()
        to_peers(job, 1)
        offers[job][2].wait_recv()
        to_peers(job, 3)

    offer(count)
    gathers[count][peer, chip] = given[...]
    first = [go([to_row(job, k) for k in rows]) for job in jobs]
    second = []
    for job in jobs:
        for c in first[job]:
            c.wait_recv()
        acc = sources[job][row].astype(F32)
        for k in rows:
            acc = acc + firsts[job][k - 1].astype(F32)
        partials[job][...] = acc.astype(partials[job].dtype)
        second.append(go([to_chip(job, k) for k in chips]))
        if job == 0:
            from_far(count)
    for job in jobs:
        for c in second[job]:
            c.wait_recv()
        acc = partials[job][chip].astype(F32)
        for k in chips:
            acc = acc + seconds[job][k - 1].astype(F32)
        gathers[job][peer, chip] = acc.astype(gathers[job].dtype)
        offer(job)
    from_near(count)
    for job in jobs:
        from_far(job)
    for job in jobs:
        from_near(job)
    for job in (count, *jobs):
        for c in passed[job]:
            c.wait_recv()
        outs[job][...] = gathers[job][...]
    for c in sent:
        c.wait_send()


def reduce_everywhere(wide, peers, narrow, arrays, quarter):
    count = len(arrays)

    def scratch(*lead):
        return [pltpu.VMEM((*lead, *a.shape[2:]), a.dtype) for a in arrays]

    copies = narrow + 2 * GROUPS - 2 + GROUPS * (peers - 1)
    in_vmem = pl.BlockSpec(memory_space=pltpu.VMEM)
    whole = (peers, GROUPS, *quarter.shape)
    return pl.pallas_call(
        functools.partial(reduce_kernel, wide, peers, narrow, count),
        name="reduce_everywhere",
        out_shape=[jax.ShapeDtypeStruct((peers, *a.shape[1:]), a.dtype) for a in arrays]
        + [jax.ShapeDtypeStruct(whole, quarter.dtype)],
        in_specs=[in_vmem] * (count + 1),
        out_specs=[in_vmem] * (count + 1),
        scratch_shapes=scratch(narrow - 1, GROUPS)
        + scratch(GROUPS)
        + scratch(GROUPS - 1)
        + scratch(peers, GROUPS)
        + [pltpu.VMEM(whole, quarter.dtype)]
        + [pltpu.SemaphoreType.DMA((count + 1, copies))] * 2,
        compiler_params=pltpu.CompilerParams(collective_id=1, has_side_effects=True),
        cost_estimate=pl.CostEstimate(
            flops=10**6, bytes_accessed=10**6, transcendentals=0
        ),
    )(*arrays, quarter)


def assembled(blocks, peers, share, pieces, everything):
    def rows_of(array):
        return array.reshape(-1, array.shape[-1])

    columns = [
        rows_of(pieces[array][p])[:, start : start + width]
        for third in range(3)
        for p in range(peers)
        for array, start, width, which in blocks
        if which == third
    ]
    fc1 = [
        everything[p, k, share : 2 * share] for p in range(peers) for k in range(GROUPS)
    ]
    out = [rows_of(everything[p, :, 2 * share :]) for p in range(peers)]
    fc2 = [rows_of(everything[p, :, :share]) for p in range(peers)]
    return [jnp.concatenate(parts, 1).astype(F32) for parts in (columns, out, fc1, fc2)]


def finish_kernel(blocks, peers, share, count, *refs):
    pieces, everything = refs[:count], refs[count]
    qkv, out, fc1, fc2 = refs[count + 1 :]
    step, width = share // GROUPS, everything.shape[-1]
    for p in range(peers):
        for k in range(GROUPS):
            some = slice(k * step, (k + 1) * step)
            columns = slice(p * width, (p + 1) * width)
            fc2[k * share : (k + 1) * share, columns] = everything[p, k, :share].astype(F32)
            start = (p * GROUPS + k) * width
            fc1[:, start : start + width] = everything[p, k, share : 2 * share].astype(F32)
            out[some, columns] = everything[p, k, 2 * share :].astype(F32)
            for third in range(3):
                place = third * D + p * (D // peers)
                for array, column, size, which in blocks:
                    if which == third:
                        qkv[some, place : place + size] = pieces[array][
                            p, k, :, column : column + size
                        ].astype(F32)
                        place += size


def finish(blocks, peers, share, pieces, everything):
    count = len(pieces)
    in_vmem = pl.BlockSpec(memory_space=pltpu.VMEM)
    shapes = [(share, 3 * D), (share, D), (share, 4 * D), (GROUPS * share, D)]
    return pl.pallas_call(
        functools.partial(finish_kernel, blocks, peers, share, count),
        name="finish",
        out_shape=[jax.ShapeDtypeStruct(shape, F32) for shape in shapes],
        in_specs=[in_vmem] * (count + 1),
        out_specs=[in_vmem] * 4,
        cost_estimate=pl.CostEstimate(
            flops=10**6, bytes_accessed=10**7, transcendentals=0
        ),
    )(*pieces, everything)


def marks_of(block_ids, geo):
    lane = lax.broadcasted_iota(jnp.int32, (geo.slots, LANES), 1) % HEAD
    number = block_ids[:, None] + 1
    key_marks = (lane == number).astype(BF16)
    query_marks = jnp.where((lane < 9) & (lane != number), FAR, 0.0).astype(BF16)
    return key_marks, query_marks


def tile_table(block_ids, own, geo):
    def present(size):
        return jnp.any(block_ids.reshape(-1, size, 1) == jnp.arange(-1, 8, dtype=jnp.int32), 1)

    shared = jnp.any(present(TILE)[:, None] & present(KEYS)[None], -1)
    places = jnp.arange(geo.slots // KEYS, dtype=jnp.int32)
    low = jnp.min(jnp.where(shared, places, geo.tiles), 1)
    high = jnp.max(jnp.where(shared, places + 1, 0), 1)
    return jnp.concatenate([own[None], low, high]).astype(jnp.int32)


def pick(parts, own, target):
    peers = len(parts)
    result = parts[0]
    for step in range(1, peers):
        result = jnp.where((target - own + peers) % peers == step, parts[step], result)
    return result


def ahead(wide, peers, step):
    return [(w, w // peers * peers + (w % peers + step) % peers) for w in range(wide)]


def per_device(
    tokens,
    segment_ids,
    cotangent,
    w_qkv,
    b_qv,
    w_out,
    b_out,
    ls_attn,
    ln1_gain,
    ln1_bias,
    ln2_gain,
    ln2_bias,
    w_fc1,
    b_fc1,
    w_fc2,
    b_fc2,
    ls_mlp,
):
    geo = Geometry(lax.axis_size("wide"), tokens.shape[3])
    wide, peers, chunk, rows, cols = geo.wide, geo.peers, geo.chunk, geo.rows, geo.cols
    own = lax.axis_index("wide") % peers

    def regroup(array):
        return lax.all_to_all(array, "wide", split_axis=0, concat_axis=0, tiled=True)

    token_rows = regroup(tokens.reshape(wide, chunk, D)).reshape(rows, D)
    cotangent, segment_ids, token_rows = lax.optimization_barrier(
        (cotangent, segment_ids, token_rows)
    )
    ids_out = jnp.broadcast_to(segment_ids.reshape(GROUPS, 1, geo.piece), (GROUPS, peers, geo.piece))
    block_ids = regroup(ids_out.reshape(wide, geo.piece)).reshape(geo.slots)
    cotangent_rows = regroup(cotangent.reshape(wide, chunk, D)).reshape(rows, D)

    my_ids = lax.dynamic_index_in_dim(
        block_ids.reshape(wide, peers, chunk), own, 1, keepdims=False
    ).reshape(rows, 1)
    valid_rows = (my_ids >= 0).astype(F32)
    key_marks, query_marks = marks_of(block_ids, geo)
    table = tile_table(block_ids, own, geo)

    bias_all = jnp.concatenate([b_qv[:D], jnp.zeros((D,), F32), b_qv[D:]])
    w_heads = w_qkv.reshape(D, 3, peers, geo.real_cols)
    b_heads = bias_all.reshape(3, peers, geo.real_cols)
    o_heads = w_out.reshape(peers, geo.real_cols, D)
    spare = cols - geo.real_cols

    w_own = lax.dynamic_index_in_dim(w_heads, own, 2, keepdims=False)
    w_own = jnp.pad(w_own, ((0, 0), (0, 0), (0, spare))).reshape(D, 3 * cols)
    b_own = lax.dynamic_index_in_dim(b_heads, own, 1, keepdims=False)
    b_own = jnp.pad(b_own, ((0, 0), (0, spare))).reshape(3 * cols)

    def outward_of(step):
        o = lax.dynamic_index_in_dim(o_heads, (own + step) % peers, 0, keepdims=False)
        return jnp.pad(o, ((0, spare), (0, 0)))

    o_parts = [outward_of(step) for step in range(peers)]

    def send(array, step):
        return lax.ppermute(array, "wide", ahead(wide, peers, step % peers))

    def peer_share(left, right):
        width = right.shape[1] // peers

        def product(step):
            start = (own + step) % peers * width
            some = lax.dynamic_slice_in_dim(right, start, width, 1)
            return lax.dot_general(left, some, (((0,), (0,)), ((), ())), preferred_element_type=F32)

        travels = [send(product(step).astype(BF16), step) for step in range(1, peers)]
        return (product(0) + sum(t.astype(F32) for t in travels)).astype(BF16)

    def scattered(array):
        return lax.psum_scatter(array, "narrow", scatter_dimension=0, tiled=True)

    def over_chips(array):
        return lax.psum(array, "wide", axis_index_groups=[
            list(range(p, wide, peers)) for p in range(peers)
        ])

    def swap_chips(array, k):
        pairs = [(w, (w // peers ^ k) * peers + w % peers) for w in range(wide)]
        return lax.ppermute(array, "wide", pairs)

    def paired(place, mine, theirs, axis):
        low, high = jnp.where(place == 0, mine, theirs), jnp.where(place == 0, theirs, mine)
        return jnp.stack([low, high], axis)

    def added(a, b):
        return (a.astype(F32) + b.astype(F32)).astype(BF16)

    def held(*values):
        return lax.optimization_barrier(values)

    def over_peers(array):
        return lax.all_gather(array, "wide", axis_index_groups=[
            list(range(g, g + peers)) for g in range(0, wide, peers)
        ])

    inputs = token_rows.astype(F32)
    normed, norm_first_back = jax.vjp(layer_norm, inputs, ln1_gain, ln1_bias)
    normed_low = normed.astype(BF16)
    normed_parts = [normed_low] + [send(normed_low, step) for step in range(1, peers)]
    qkv_parts = [
        (dot_nn(part, w_own) + b_own).astype(BF16).reshape(wide, chunk, 3 * cols)
        for part in normed_parts
    ]
    *mixed_parts, lse = attend(geo, table, qkv_parts, key_marks, query_marks)
    mixed_parts, cotangent_rows = lax.optimization_barrier((mixed_parts, cotangent_rows))
    mixed_home = [
        (send(part, -step) if step else part).reshape(rows, cols)
        for step, part in enumerate(mixed_parts)
    ]
    mixed_rows = jnp.concatenate(mixed_home, 1)
    w_out_rel = jnp.concatenate(o_parts, 0)
    projected = dot_nn(mixed_rows, w_out_rel) + b_out
    hidden = inputs + ls_attn * projected
    second, norm_second_back = jax.vjp(layer_norm, hidden, ln2_gain, ln2_bias)
    second_low = second.astype(BF16)
    pre_act = dot_nn(second_low, w_fc1) + b_fc1
    activation, gelu_back = jax.vjp(gelu_exact, pre_act)
    act_low = activation.astype(BF16)
    mlp_out = dot_nn(act_low, w_fc2) + b_fc2
    result = (hidden + ls_mlp * mlp_out).astype(BF16)
    output = regroup(result.reshape(wide, chunk, D)).reshape(tokens.shape)
    grad_out = cotangent_rows.astype(F32) * valid_rows
    grad_ls_mlp = jnp.sum(grad_out * mlp_out, 0)
    grad_mlp = (ls_mlp * grad_out).astype(BF16)
    grad_b_fc2 = jnp.sum(grad_mlp.astype(F32), 0)
    grad_w_fc2 = peer_share(act_low, grad_mlp)
    grad_act = jnp.dot(grad_mlp, w_fc2.T, preferred_element_type=F32)
    grad_pre = gelu_back(grad_act)[0].astype(BF16)
    grad_pre, grad_w_fc2 = lax.optimization_barrier((grad_pre, grad_w_fc2))
    sums_fc2 = scattered(grad_w_fc2)
    grad_b_fc1 = jnp.sum(grad_pre.astype(F32), 0)
    grad_w_fc1 = peer_share(second_low, grad_pre)
    grad_second = jnp.dot(grad_pre, w_fc1.T, preferred_element_type=F32)
    grad_hidden_norm, grad_ln2_gain, grad_ln2_bias = norm_second_back(grad_second)
    grad_hidden = grad_out + grad_hidden_norm
    grad_ls_attn = jnp.sum(grad_hidden * projected, 0)
    grad_proj = (ls_attn * grad_hidden).astype(BF16)
    grad_b_out = jnp.sum(grad_proj.astype(F32), 0)
    proj_parts = [grad_proj] + [send(grad_proj, step) for step in range(1, peers)]
    mixed_plain = jnp.concatenate(
        [pick([m[:, : geo.real_cols] for m in mixed_home], own, g) for g in range(peers)], 1
    )
    grad_w_out = peer_share(mixed_plain, grad_proj)
    grad_parts = [
        jnp.dot(part, o_parts[0].T, preferred_element_type=F32)
        .astype(BF16)
        .reshape(wide, chunk, cols)
        for part in proj_parts
    ]
    narrow = lax.axis_size("narrow")
    wide_half = grad_w_fc1.shape[1]

    def side_by_side(array):
        return jnp.concatenate([array[:, k] for k in range(array.shape[1])], -1)

    grad_w_both = jnp.concatenate(
        [
            grad_w_fc1.reshape(narrow, -1, wide_half),
            side_by_side(grad_w_out.reshape(narrow, GROUPS, -1, grad_w_out.shape[1])),
        ],
        1,
    ).reshape(-1, wide_half)
    grad_parts, grad_w_both, sums_fc2 = lax.optimization_barrier(
        (grad_parts, grad_w_both, sums_fc2)
    )
    sums_both = scattered(grad_w_both)

    share, step_width = D // narrow, D // peers
    chip = lax.axis_index("wide") // peers
    near, far = chip % 2, chip // 2
    begins = [0, geo.pairs - 1] if geo.pairs > 1 else [0]
    counts = [end - begin for begin, end in zip(begins, [*begins[1:], geo.pairs])]

    def back(index):
        return attend_back(
            geo,
            begins[index],
            counts[index],
            table,
            qkv_parts,
            grad_parts,
            mixed_parts,
            lse,
            key_marks,
            query_marks,
        )

    calls = [back(0)]
    quarters = jnp.stack(
        [sums_both[:, k * step_width : (k + 1) * step_width] for k in range(GROUPS)]
    )
    quarters = jnp.concatenate([sums_fc2.reshape(GROUPS, share, step_width), quarters], 1)
    quarters, calls = held(quarters, calls)
    quarters = quarters.reshape(2, 2, -1, step_width)
    going = lax.dynamic_index_in_dim(quarters, 1 - near, 1, keepdims=False)
    staying = lax.dynamic_index_in_dim(quarters, near, 1, keepdims=False)
    going, staying, grad_parts, calls = held(going, staying, grad_parts, calls)
    came = swap_chips(going, 1)
    calls += [back(index) for index in range(1, len(begins))]
    came, calls, output = held(came, calls, output)
    halves = added(staying, came)
    going = lax.dynamic_index_in_dim(halves, 1 - far, 0, keepdims=False)
    staying = lax.dynamic_index_in_dim(halves, far, 0, keepdims=False)
    going, staying, calls = held(going, staying, calls)
    came = swap_chips(going, 2)
    output = jnp.where(segment_ids[..., None] >= 0, output, jnp.zeros_like(output))
    calls = [[part.reshape(rows, -1) for part in made] for made in calls]
    w_split = w_own.reshape(D, 3, geo.pairs, LANES)
    w_calls = [
        w_split[:, :, begin : begin + count].reshape(D, -1)
        for begin, count in zip(begins, counts)
    ]
    partial = [
        sum(
            jnp.dot(made[back], w.T, preferred_element_type=F32)
            for made, w in zip(calls, w_calls)
        )
        for back in range(peers)
    ]
    for step in range(1, peers):
        partial[step] = send(partial[step].astype(BF16), -step)
    grad_normed = partial[0]
    for step in range(1, peers):
        grad_normed = grad_normed + partial[step].astype(F32)
    sums = [
        sum(jnp.sum(part.astype(F32), 0) for part in made).reshape(3, 1, -1) for made in calls
    ]
    sums = jnp.concatenate(sums, 2)[:, :, : geo.real_cols]
    sums = jnp.where(jnp.arange(peers)[:, None] == own, sums, 0.0)
    grad_b_qv = sums[::2].reshape(2 * D)
    grad_inputs_norm, grad_ln1_gain, grad_ln1_bias = norm_first_back(grad_normed)
    grad_rows = (grad_hidden + grad_inputs_norm).astype(BF16)
    grad_rows, calls = held(grad_rows, calls)
    grad_w_qkv = []
    for made, count in zip(calls, counts):
        weight = sum(
            jnp.einsum("td,te->de", a, b, preferred_element_type=F32)
            for a, b in zip(normed_parts, made)
        ).astype(BF16)
        grad_w_qkv += [weight[:, k * 3 * LANES : (k + 1) * 3 * LANES] for k in range(count)]
    grad_tokens = regroup(grad_rows.reshape(wide, chunk, D)).reshape(tokens.shape)

    vectors = [
        grad_b_qv,
        grad_b_out,
        grad_ls_attn,
        grad_ln1_gain,
        grad_ln1_bias,
        grad_ln2_gain,
        grad_ln2_bias,
        grad_b_fc1,
        grad_b_fc2,
        grad_ls_mlp,
    ]
    flat = jnp.concatenate([v.reshape(narrow, -1) for v in vectors], 1)
    flat = jnp.pad(flat, ((0, 0), (0, -flat.shape[1] % (GROUPS * 8 * LANES))))
    flat = flat.reshape(narrow, GROUPS, -1, LANES)
    thirds = [w.reshape(narrow, GROUPS, -1, 3 * LANES) for w in grad_w_qkv]
    came, flat, thirds = held(came, flat, thirds)
    quarter = added(staying, came)
    if narrow <= GROUPS:
        flat, *thirds, everything = reduce_everywhere(
            wide, peers, narrow, [flat, *thirds], quarter
        )
    else:
        came = swap_chips(quarter, 2)
        pair = paired(far, quarter, came, 0)
        whole_share = paired(near, pair, swap_chips(pair, 1), 1)
        whole_share = whole_share.reshape(GROUPS, -1, step_width)
        everything = over_peers(whole_share)
        flat, *thirds = (
            over_peers(over_chips(scattered(a))).reshape(peers, *a.shape[1:])
            for a in (flat, *thirds)
        )

    flat = sum(flat[p] for p in range(peers)).reshape(-1)
    small, start = [], 0
    for v in vectors:
        size = v.shape[0] // narrow
        small.append(flat[start : start + size])
        start += size
    blocks = []
    for third in range(3):
        for begin, count in zip(begins, counts):
            for pair in range(begin, begin + count):
                array, column = divmod(third * count + pair - begin, 3)
                width = min(LANES, geo.real_cols - pair * LANES)
                blocks.append((begin + array, column * LANES, width, third))
    if narrow <= GROUPS:
        matrices = finish(blocks, peers, share, thirds, everything)
    else:
        matrices = assembled(blocks, peers, share, thirds, everything)
    done_qkv, done_out, done_fc1, done_fc2 = matrices

    return (
        output,
        grad_tokens,
        done_qkv,
        small[0],
        done_out,
        small[1],
        small[2],
        small[3],
        small[4],
        small[5],
        small[6],
        done_fc1,
        small[7],
        done_fc2,
        small[8],
        small[9],
    )


def solution(mesh):
    rows = P("narrow", "wide", None, None, None)
    placed = (rows, P("narrow", "wide", None, None), rows) + (P(),) * 14
    matrix, vector = P("narrow", None), P("narrow")
    return jax.shard_map(
        per_device,
        mesh=mesh,
        in_specs=placed,
        out_specs=(
            rows,
            rows,
            matrix,
            vector,
            matrix,
            vector,
            vector,
            vector,
            vector,
            vector,
            vector,
            matrix,
            vector,
            matrix,
            vector,
            vector,
        ),
        check_vma=False,
    )
```

```python
import functools
import jax
import jax.numpy as jnp
from jax import lax
from jax.experimental import pallas as pl
from jax.experimental.pallas import tpu as pltpu
from jax.sharding import PartitionSpec as P

D = 768
HEADS = 12
HEAD = 64
GROUPS = 4
TILE = 512
KEYS = 512
LANES = 128
EPSILON = 1e-06
ROOT_HALF = 0.7071067811865476
FAR = -1e30
F32 = jnp.float32
BF16 = jnp.bfloat16


def layer_norm(values, gain, bias):
    average = jnp.mean(values, -1, keepdims=True)
    centred = values - average
    variance = jnp.mean(centred * centred, -1, keepdims=True)
    return centred * lax.rsqrt(variance + EPSILON) * gain + bias


def gelu_exact(values):
    return 0.5 * values * (1.0 + lax.erf(values * ROOT_HALF))


def dot_nt(a, b):
    return lax.dot_general(a, b, (((1,), (1,)), ((), ())), preferred_element_type=F32)


def dot_nn(a, b):
    return jnp.dot(a, b, preferred_element_type=F32)


class Geometry:
    def __init__(self, wide, piece):
        self.wide = wide
        self.piece = piece
        self.peers = wide // GROUPS
        self.chunk = piece // self.peers
        self.rows = wide * self.chunk
        self.slots = wide * piece
        heads = HEADS // self.peers
        self.real_cols = heads * HEAD
        self.pairs = (heads + 1) // 2
        self.cols = self.pairs * LANES
        self.tiles = self.slots // TILE


def gather_rows(geo, own, parts, column, fill):
    for back, part in enumerate(parts):
        source = lax.rem(own - back + geo.peers, geo.peers)
        for span in range(geo.wide):
            offset = pl.multiple_of(span * geo.piece + source * geo.chunk, geo.chunk)
            fill(offset, part[span, :, pl.ds(pl.multiple_of(column, LANES), LANES)])


def scatter_rows(geo, own, parts, column, source_ref):
    for back, part in enumerate(parts):
        source = lax.rem(own - back + geo.peers, geo.peers)
        for span in range(geo.wide):
            offset = pl.multiple_of(span * geo.piece + source * geo.chunk, geo.chunk)
            part[span, :, pl.ds(pl.multiple_of(column, LANES), LANES)] = source_ref[
                pl.ds(offset, geo.chunk), :
            ]


def attend_kernel(geo, table, *refs):
    peers = geo.peers
    qkv = refs[:peers]
    key_marks, query_marks = refs[peers : peers + 2]
    mixed = refs[peers + 2 : 2 * peers + 2]
    lse = refs[2 * peers + 2]
    ka, qa, va, ob, worst = refs[2 * peers + 3 :]
    pair = pl.program_id(0)
    own = table[0]
    first = lax.broadcasted_iota(jnp.int32, (geo.chunk, LANES), 1) < HEAD
    left = lax.broadcasted_iota(jnp.int32, (TILE, LANES), 1) < HEAD
    one = jnp.ones((geo.chunk, LANES), BF16)
    picks = lax.broadcasted_iota(jnp.int32, (8, LANES), 1) == HEAD * lax.broadcasted_iota(
        jnp.int32, (8, LANES), 0
    )

    def put_query(offset, values):
        marks = query_marks[pl.ds(offset, geo.chunk), :]
        scaled = values * 0.125
        qa[0, pl.ds(offset, geo.chunk), :] = jnp.where(first, scaled, marks)
        qa[1, pl.ds(offset, geo.chunk), :] = jnp.where(first, marks, scaled)

    def put_key(offset, values):
        marks = key_marks[pl.ds(offset, geo.chunk), :]
        ka[0, pl.ds(offset, geo.chunk), :] = jnp.where(first, values, marks)
        ka[1, pl.ds(offset, geo.chunk), :] = jnp.where(first, marks, values)

    def put_value(offset, values):
        va[0, pl.ds(offset, geo.chunk), :] = jnp.where(first, values, one)
        va[1, pl.ds(offset, geo.chunk), :] = jnp.where(first, one, values)

    gather_rows(geo, own, qkv, pair * LANES, put_query)
    gather_rows(geo, own, qkv, geo.cols + pair * LANES, put_key)
    gather_rows(geo, own, qkv, 2 * geo.cols + pair * LANES, put_value)

    def scores(which, step, at):
        return dot_nt(qa[which, pl.ds(at, TILE), :], ka[which, pl.ds(step, KEYS), :])

    def weighted(which, step, p):
        return dot_nn(p.astype(BF16), va[which, pl.ds(step, KEYS), :])

    def store(at, acc0, acc1, m0, m1):
        totals = pltpu.roll(jnp.where(left, acc1, acc0), HEAD, 1)
        ob[pl.ds(at, TILE), :] = (jnp.where(left, acc0, acc1) / totals).astype(BF16)
        logs = jnp.log(totals) + jnp.where(left, m0, m1)
        lse[0, :, pl.ds(at, TILE)] = lax.dot_general(
            picks.astype(F32),
            logs,
            (((1,), (1,)), ((), ())),
            precision=lax.Precision.HIGHEST,
            preferred_element_type=F32,
        )
        return totals

    def plain_tile(tile, _):
        at = pl.multiple_of(tile * TILE, TILE)

        def key_tile(index, carry):
            acc0, acc1 = carry
            step = pl.multiple_of(index * KEYS, KEYS)
            p0 = jnp.exp(scores(0, step, at))
            p1 = jnp.exp(scores(1, step, at))
            return acc0 + weighted(0, step, p0), acc1 + weighted(1, step, p1)

        blank = jnp.zeros((TILE, LANES), F32)
        acc0, acc1 = lax.fori_loop(
            table[1 + tile], table[1 + geo.tiles + tile], key_tile, (blank, blank)
        )
        totals = store(at, acc0, acc1, 0.0, 0.0)
        odd = jnp.where((totals > 1e-20) & (totals < 1e20), 0.0, 1.0)
        worst[...] = jnp.maximum(worst[...], jnp.max(odd.reshape(TILE // 8, 8, LANES), 0))
        return 0

    def careful_tile(tile, _):
        at = pl.multiple_of(tile * TILE, TILE)

        def one_head(which, step, m, acc):
            s = scores(which, step, at)
            m_new = jnp.maximum(m, jnp.max(s, 1, keepdims=True))
            acc = acc * jnp.exp(m - m_new) + weighted(which, step, jnp.exp(s - m_new))
            return m_new, acc

        def key_tile(index, carry):
            step = pl.multiple_of(index * KEYS, KEYS)
            return (*one_head(0, step, *carry[:2]), *one_head(1, step, *carry[2:]))

        low = jnp.full((TILE, 1), -2e30, F32)
        blank = jnp.zeros((TILE, LANES), F32)
        m0, acc0, m1, acc1 = lax.fori_loop(
            table[1 + tile], table[1 + geo.tiles + tile], key_tile, (low, blank, low, blank)
        )
        store(at, acc0, acc1, m0, m1)
        return 0

    worst[...] = jnp.zeros_like(worst)
    lax.fori_loop(0, geo.tiles, plain_tile, 0)

    @pl.when(jnp.max(worst[...]) > 0.0)
    def _():
        lax.fori_loop(0, geo.tiles, careful_tile, 0)

    scatter_rows(geo, own, mixed, pair * LANES, ob)


def attend_back_kernel(geo, begin, count, table, *refs):
    peers = geo.peers
    qkv = refs[:peers]
    grads = refs[peers : 2 * peers]
    mixed = refs[2 * peers : 3 * peers]
    lse, key_marks, query_marks = refs[3 * peers : 3 * peers + 3]
    outs = refs[3 * peers + 3 : 4 * peers + 3]
    ka, qa, vn, qm, dm, kn, kt, dk, dv, ob, inner = refs[4 * peers + 3 :]
    step_pair = pl.program_id(0)
    pair = begin + step_pair
    own = table[0]
    lane = lax.broadcasted_iota(jnp.int32, (geo.chunk, LANES), 1)
    first = lane < HEAD
    zero = jnp.zeros((geo.chunk, LANES), BF16)
    half = lax.broadcasted_iota(jnp.int32, (8, LANES), 1) // HEAD == lax.broadcasted_iota(
        jnp.int32, (8, LANES), 0
    )
    half = half.astype(BF16)

    def put_query(offset, values):
        marks = query_marks[pl.ds(offset, geo.chunk), :]
        scaled = values * 0.125
        qa[0, pl.ds(offset, geo.chunk), :] = jnp.where(first, scaled, marks)
        qa[1, pl.ds(offset, geo.chunk), :] = jnp.where(first, marks, scaled)
        qm[0, pl.ds(offset, geo.chunk), :] = jnp.where(first, scaled, zero)
        qm[1, pl.ds(offset, geo.chunk), :] = jnp.where(first, zero, scaled)

    def put_key(offset, values):
        marks = key_marks[pl.ds(offset, geo.chunk), :]
        ka[0, pl.ds(offset, geo.chunk), :] = jnp.where(first, values, marks)
        ka[1, pl.ds(offset, geo.chunk), :] = jnp.where(first, marks, values)
        kn[pl.ds(offset, geo.chunk), :] = values

    def put_value(offset, values):
        vn[pl.ds(offset, geo.chunk), :] = values

    def put_mixed(offset, values):
        ob[pl.ds(offset, geo.chunk), :] = values

    def put_grad(offset, values):
        dm[0, pl.ds(offset, geo.chunk), :] = jnp.where(first, values, zero)
        dm[1, pl.ds(offset, geo.chunk), :] = jnp.where(first, zero, values)
        product = values.astype(F32) * ob[pl.ds(offset, geo.chunk), :].astype(F32)
        high = product.astype(BF16)
        rest = (product - high.astype(F32)).astype(BF16)
        kn[pl.ds(offset, geo.chunk), :] = high
        vn[pl.ds(offset, geo.chunk), :] = rest

    gather_rows(geo, own, mixed, pair * LANES, put_mixed)
    gather_rows(geo, own, grads, pair * LANES, put_grad)
    for tile in range(geo.tiles):
        rows = slice(tile * TILE, (tile + 1) * TILE)
        inner[:, rows] = dot_nt(half, kn[rows, :]) + dot_nt(half, vn[rows, :])
    gather_rows(geo, own, qkv, pair * LANES, put_query)
    gather_rows(geo, own, qkv, geo.cols + pair * LANES, put_key)
    gather_rows(geo, own, qkv, 2 * geo.cols + pair * LANES, put_value)
    for tile in range(geo.tiles):
        rows = slice(tile * TILE, (tile + 1) * TILE)
        kt[:, rows] = kn[rows, :].T
    dk[...] = jnp.zeros_like(dk)
    dv[...] = jnp.zeros_like(dv)

    def query_tile(tile, _):
        at = pl.multiple_of(tile * TILE, TILE)

        def one(which, step):
            s = dot_nt(ka[which, pl.ds(step, KEYS), :], qa[which, pl.ds(at, TILE), :])
            p = jnp.exp(s - lse[0, which : which + 1, pl.ds(at, TILE)])
            g = dot_nt(vn[pl.ds(step, KEYS), :], dm[which, pl.ds(at, TILE), :])
            ds = (p * (g - inner[which : which + 1, pl.ds(at, TILE)])).astype(BF16)
            return p.astype(BF16), ds

        def key_tile(index, carry):
            a0, a1 = carry
            step = pl.multiple_of(index * KEYS, KEYS)
            p0, s0 = one(0, step)
            p1, s1 = one(1, step)
            dv[pl.ds(step, KEYS), :] += dot_nn(p0, dm[0, pl.ds(at, TILE), :]) + dot_nn(
                p1, dm[1, pl.ds(at, TILE), :]
            )
            dk[pl.ds(step, KEYS), :] += dot_nn(s0, qm[0, pl.ds(at, TILE), :]) + dot_nn(
                s1, qm[1, pl.ds(at, TILE), :]
            )
            a0 = a0 + dot_nn(kt[:HEAD, pl.ds(step, KEYS)], s0)
            a1 = a1 + dot_nn(kt[HEAD:, pl.ds(step, KEYS)], s1)
            return a0, a1

        blank = jnp.zeros((HEAD, TILE), F32)
        a0, a1 = lax.fori_loop(
            table[1 + tile], table[1 + geo.tiles + tile], key_tile, (blank, blank)
        )
        ob[pl.ds(at, TILE), :] = (jnp.concatenate([a0, a1], 0) * 0.125).T.astype(BF16)
        return 0

    lax.fori_loop(0, geo.tiles, query_tile, 0)
    scatter_rows(geo, own, outs, step_pair * LANES, ob)
    ob[...] = dk[...].astype(BF16)
    scatter_rows(geo, own, outs, (count + step_pair) * LANES, ob)
    ob[...] = dv[...].astype(BF16)
    scatter_rows(geo, own, outs, (2 * count + step_pair) * LANES, ob)


def whole_spec(shape):
    return pl.BlockSpec(shape, lambda pair, table: (0,) * len(shape))


def attend(geo, table, qkv_parts, key_marks, query_marks):
    out_shape = [
        jax.ShapeDtypeStruct((geo.wide, geo.chunk, geo.cols), BF16) for _ in range(geo.peers)
    ] + [jax.ShapeDtypeStruct((geo.pairs, 8, geo.slots), F32)]
    return pl.pallas_call(
        functools.partial(attend_kernel, geo),
        name="attend",
        out_shape=out_shape,
        grid_spec=pltpu.PrefetchScalarGridSpec(
            num_scalar_prefetch=1,
            grid=(geo.pairs,),
            in_specs=[whole_spec(a.shape) for a in qkv_parts]
            + [whole_spec((geo.slots, LANES))] * 2,
            out_specs=[whole_spec((geo.wide, geo.chunk, geo.cols))] * geo.peers
            + [pl.BlockSpec((1, 8, geo.slots), lambda pair, table: (pair, 0, 0))],
            scratch_shapes=[
                pltpu.VMEM((2, geo.slots, LANES), BF16),
                pltpu.VMEM((2, geo.slots, LANES), BF16),
                pltpu.VMEM((2, geo.slots, LANES), BF16),
                pltpu.VMEM((geo.slots, LANES), BF16),
                pltpu.VMEM((8, LANES), F32),
            ],
        ),
        cost_estimate=pl.CostEstimate(
            flops=4 * geo.slots * geo.slots * geo.real_cols,
            transcendentals=geo.slots * geo.slots * 6,
            bytes_accessed=4 * geo.slots * geo.cols * 2,
        ),
    )(table, *qkv_parts, key_marks, query_marks)


def attend_back(geo, begin, count, table, qkv_parts, grad_parts, mixed_parts, lse, key_marks, query_marks):
    wide_shape = (geo.wide, geo.chunk, 3 * count * LANES)
    two = pltpu.VMEM((2, geo.slots, LANES), BF16)
    one = pltpu.VMEM((geo.slots, LANES), BF16)
    return pl.pallas_call(
        functools.partial(attend_back_kernel, geo, begin, count),
        name=f"attend_back_{begin}",
        out_shape=[jax.ShapeDtypeStruct(wide_shape, BF16) for _ in range(geo.peers)],
        grid_spec=pltpu.PrefetchScalarGridSpec(
            num_scalar_prefetch=1,
            grid=(count,),
            in_specs=[whole_spec(a.shape) for a in (*qkv_parts, *grad_parts, *mixed_parts)]
            + [pl.BlockSpec((1, 8, geo.slots), lambda pair, table: (begin + pair, 0, 0))]
            + [whole_spec((geo.slots, LANES))] * 2,
            out_specs=[whole_spec(wide_shape)] * geo.peers,
            scratch_shapes=[two, two, one, two, two, one]
            + [
                pltpu.VMEM((LANES, geo.slots), BF16),
                pltpu.VMEM((geo.slots, LANES), F32),
                pltpu.VMEM((geo.slots, LANES), F32),
                one,
                pltpu.VMEM((8, geo.slots), F32),
            ],
        ),
        cost_estimate=pl.CostEstimate(
            flops=10 * geo.slots * geo.slots * count * LANES,
            transcendentals=geo.slots * geo.slots * 2 * count,
            bytes_accessed=12 * geo.slots * geo.cols * 2,
        ),
    )(table, *qkv_parts, *grad_parts, *mixed_parts, lse, key_marks, query_marks)


def flipped(place, k):
    bits = [place // 2**b % 2 for b in range(6)]
    return sum((1 - bit if k >> b & 1 else bit) * 2**b for b, bit in enumerate(bits))


def reduce_kernel(wide, peers, narrow, shares, *refs):
    count = 1 + sum(shares)
    flat, lefts = refs[0], refs[1 : peers + 1]
    rights = refs[peers + 1 : peers + 1 + peers * len(shares)]
    refs = refs[peers + 1 + peers * len(shares) :]
    given, outs = refs[0], refs[1 : count + 2]
    scratch = refs[count + 2 :]
    products, turned = scratch[: count - 1], scratch[count - 1]
    scratch = scratch[count:]
    firsts, partials, seconds = (scratch[k * count : (k + 1) * count] for k in range(3))
    gathers = scratch[3 * count : 4 * count + 1]
    halves, sums, quarter, send_sems, recv_sems = scratch[4 * count + 1 :]
    row = lax.axis_index("narrow")
    mine = lax.axis_index("wide")
    chip, peer = mine // peers, mine % peers

    barrier = pltpu.get_barrier_semaphore()
    for k in range(1, narrow):
        pl.semaphore_signal(
            barrier,
            inc=1,
            device_id={"narrow": flipped(row, k)},
            device_id_type=pl.DeviceIdType.MESH,
        )
    for k in range(1, wide):
        pl.semaphore_signal(
            barrier,
            inc=1,
            device_id={"wide": flipped(mine, k)},
            device_id_type=pl.DeviceIdType.MESH,
        )
    pl.semaphore_wait(barrier, narrow - 1 + wide - 1)

    def copy(job, index, source, target, device):
        return pltpu.make_async_remote_copy(
            src_ref=source,
            dst_ref=target,
            send_sem=send_sems.at[job, index],
            recv_sem=recv_sems.at[job, index],
            device_id=device,
            device_id_type=pl.DeviceIdType.MESH,
        )

    def to_row(job, k):
        target = flipped(row, k)
        source = products[job - 1].at[k] if job else flat.at[target]
        return copy(job, k - 1, source, firsts[job].at[k - 1], {"narrow": target})

    def multiply(job, k):
        number, column = job - 1, 0
        for call, held in enumerate(shares):
            if number < held:
                column = number * 3 * LANES
                break
            number -= held
        size = turned.shape[1] // narrow
        start = pl.multiple_of(flipped(row, k) * size, size)
        total = sum(
            dot_nn(
                turned[p, pl.ds(start, size), :],
                rights[call * peers + p][:, column : column + 3 * LANES],
            )
            for p in range(peers)
        )
        step = size // GROUPS
        for part in range(GROUPS):
            products[job - 1][k, part] = total[part * step : (part + 1) * step].astype(BF16)

    def to_chip(job, k):
        target = flipped(chip, k)
        return copy(
            job,
            narrow - 2 + k,
            partials[job].at[target],
            seconds[job].at[k - 1],
            {"wide": target * peers + peer},
        )

    rows, chips, others = range(1, narrow), range(1, GROUPS), range(1, peers)
    after_chips = narrow + GROUPS - 2
    near, far = flipped(chip, 1), flipped(chip, 2)

    def place(job, k):
        return gathers[job].at[peer, flipped(chip, k)]

    def to_far(job):
        return copy(job, after_chips, place(job, 0), place(job, 0), {"wide": far * peers + peer})

    def to_near(job):
        return copy(job, after_chips + 1, place(job, 0), place(job, 0), {"wide": near * peers + peer})

    def relay(job):
        target = {"wide": near * peers + peer}
        return copy(job, after_chips + 2, place(job, 2), place(job, 2), target)

    sent, passed = [], [[] for _ in gathers]

    def go(copies):
        for c in copies:
            c.start()
        sent.extend(copies)
        return copies

    def to_peers(job, k):
        source = place(job, k)
        passed[job] += go(
            [
                copy(
                    job,
                    after_chips + 3 + k * (peers - 1) + other - 1,
                    source,
                    place(job, k),
                    {"wide": chip * peers + flipped(peer, other)},
                )
                for other in others
            ]
        )

    jobs = range(count)
    offers = {}

    def offer(job):
        offers[job] = go([to_far(job), to_near(job)])
        to_peers(job, 0)

    def from_far(job):
        offers[job][0].wait_recv()
        offers[job] += go([relay(job)])
        to_peers(job, 2)

    def from_near(job):
        offers[job][1].wait_recv()
        to_peers(job, 1)
        offers[job][2].wait_recv()
        to_peers(job, 3)

    nearby = {"wide": near * peers + peer}
    distant = {"wide": far * peers + peer}
    swapped = go(
        [
            copy(count, 0, given.at[near], halves.at[0], nearby),
            copy(count, 1, given.at[flipped(chip, 3)], halves.at[1], nearby),
        ]
    )
    first = [go([to_row(0, k) for k in rows])]
    for p in range(peers):
        for start in range(0, turned.shape[1], LANES):
            turned[p, start : start + LANES, :] = lefts[p][:, start : start + LANES].T
    for job in range(1, count):
        first.append([])
        for k in rows:
            multiply(job, k)
            first[job] += go([to_row(job, k)])
        multiply(job, 0)
        if job == 1:
            for c in swapped:
                c.wait_recv()
            sums[1] = (given[far].astype(F32) + halves[1].astype(F32)).astype(BF16)
            swapped += go([copy(count, 2, sums.at[1], quarter, distant)])
            sums[0] = (given[chip].astype(F32) + halves[0].astype(F32)).astype(BF16)
    second = []
    for job in jobs:
        for c in first[job]:
            c.wait_recv()
        acc = products[job - 1][0].astype(F32) if job else flat[row]
        for k in rows:
            acc = acc + firsts[job][k - 1].astype(F32)
        partials[job][...] = acc.astype(partials[job].dtype)
        second.append(go([to_chip(job, k) for k in chips]))
        if job == 1:
            swapped[2].wait_recv()
            final = sums[0].astype(F32) + quarter[...].astype(F32)
            gathers[count][peer, chip] = final.astype(BF16)
            offer(count)
    for job in jobs:
        for c in second[job]:
            c.wait_recv()
        acc = partials[job][chip].astype(F32)
        for k in chips:
            acc = acc + seconds[job][k - 1].astype(F32)
        gathers[job][peer, chip] = acc.astype(gathers[job].dtype)
        offer(job)
    from_far(count)
    for job in jobs:
        from_far(job)
    from_near(count)
    for job in jobs:
        from_near(job)
    for job in (count, *jobs):
        for c in passed[job]:
            c.wait_recv()
        outs[job][...] = gathers[job][...]
    for c in sent:
        c.wait_send()


def reduce_everywhere(wide, peers, narrow, flat, lefts, rights, quarters):
    shares = [parts[0].shape[1] // (3 * LANES) for parts in rights]
    count = 1 + sum(shares)
    rows, depth = lefts[0].shape
    product = (GROUPS, depth // narrow // GROUPS, 3 * LANES)
    shapes = [(flat.shape[1:], F32)] + [(product, BF16)] * (count - 1)
    inputs = [flat, *lefts, *[part for parts in rights for part in parts], quarters]

    def scratch(*lead, quarters=1):
        return [
            pltpu.VMEM((*lead, *shape[1 - quarters :]), dtype) for shape, dtype in shapes
        ]

    copies = narrow + 2 * GROUPS - 2 + GROUPS * (peers - 1)
    in_vmem = pl.BlockSpec(memory_space=pltpu.VMEM)
    whole, one = (peers, *quarters.shape), quarters.shape[1:]
    return pl.pallas_call(
        functools.partial(reduce_kernel, wide, peers, narrow, shares),
        name="reduce_everywhere",
        out_shape=[jax.ShapeDtypeStruct((peers, *shape), dtype) for shape, dtype in shapes]
        + [jax.ShapeDtypeStruct(whole, BF16)],
        in_specs=[in_vmem] * len(inputs),
        out_specs=[in_vmem] * (count + 1),
        scratch_shapes=[pltpu.VMEM((narrow, *product), BF16)] * (count - 1)
        + [pltpu.VMEM((peers, depth, rows), BF16)]
        + scratch(narrow - 1)
        + scratch()
        + scratch(GROUPS - 1, quarters=0)
        + scratch(peers)
        + [pltpu.VMEM(shape, BF16) for shape in (whole, (2, *one), (2, *one), one)]
        + [pltpu.SemaphoreType.DMA((count + 1, copies))] * 2,
        compiler_params=pltpu.CompilerParams(collective_id=1, has_side_effects=True),
        cost_estimate=pl.CostEstimate(
            flops=10**6, bytes_accessed=10**6, transcendentals=0
        ),
    )(*inputs)


def assembled(blocks, peers, share, pieces, everything):
    def rows_of(array):
        return array.reshape(-1, array.shape[-1])

    columns = [
        rows_of(pieces[array][p])[:, start : start + width]
        for third in range(3)
        for p in range(peers)
        for array, start, width, which in blocks
        if which == third
    ]
    fc1 = [
        everything[p, k, share : 2 * share] for p in range(peers) for k in range(GROUPS)
    ]
    out = [rows_of(everything[p, :, 2 * share :]) for p in range(peers)]
    fc2 = [rows_of(everything[p, :, :share]) for p in range(peers)]
    return [jnp.concatenate(parts, 1).astype(F32) for parts in (columns, out, fc1, fc2)]


def finish_kernel(blocks, peers, share, count, *refs):
    pieces, everything = refs[:count], refs[count]
    kept = (len(refs) - count - 5) // 2
    qkv, out, fc1, fc2 = refs[count + 1 + kept : count + 5 + kept]
    for source, target in zip(refs[count + 1 : count + 1 + kept], refs[count + 5 + kept :]):
        target[...] = source[...]
    step, width = share // GROUPS, everything.shape[-1]
    for p in range(peers):
        for k in range(GROUPS):
            some = slice(k * step, (k + 1) * step)
            columns = slice(p * width, (p + 1) * width)
            fc2[k * share : (k + 1) * share, columns] = everything[p, k, :share].astype(F32)
            start = (p * GROUPS + k) * width
            fc1[:, start : start + width] = everything[p, k, share : 2 * share].astype(F32)
            out[some, columns] = everything[p, k, 2 * share :].astype(F32)
            for third in range(3):
                place = third * D + p * (D // peers)
                for array, column, size, which in blocks:
                    if which == third:
                        qkv[some, place : place + size] = pieces[array][
                            p, k, :, column : column + size
                        ].astype(F32)
                        place += size


def finish(blocks, peers, share, pieces, everything, *kept):
    count = len(pieces)
    in_vmem = pl.BlockSpec(memory_space=pltpu.VMEM)
    shapes = [(share, 3 * D), (share, D), (share, 4 * D), (GROUPS * share, D)]
    return pl.pallas_call(
        functools.partial(finish_kernel, blocks, peers, share, count),
        name="finish",
        out_shape=[jax.ShapeDtypeStruct(shape, F32) for shape in shapes]
        + [jax.ShapeDtypeStruct(a.shape, a.dtype) for a in kept],
        in_specs=[in_vmem] * (count + 1 + len(kept)),
        out_specs=[in_vmem] * (4 + len(kept)),
        cost_estimate=pl.CostEstimate(
            flops=10**6, bytes_accessed=10**7, transcendentals=0
        ),
    )(*pieces, everything, *kept)


def marks_of(block_ids, geo):
    lane = lax.broadcasted_iota(jnp.int32, (geo.slots, LANES), 1) % HEAD
    number = block_ids[:, None] + 1
    key_marks = (lane == number).astype(BF16)
    query_marks = jnp.where((lane < 9) & (lane != number), FAR, 0.0).astype(BF16)
    return key_marks, query_marks


def tile_table(block_ids, own, geo):
    def present(size):
        return jnp.any(block_ids.reshape(-1, size, 1) == jnp.arange(-1, 8, dtype=jnp.int32), 1)

    shared = jnp.any(present(TILE)[:, None] & present(KEYS)[None], -1)
    places = jnp.arange(geo.slots // KEYS, dtype=jnp.int32)
    low = jnp.min(jnp.where(shared, places, geo.tiles), 1)
    high = jnp.max(jnp.where(shared, places + 1, 0), 1)
    return jnp.concatenate([own[None], low, high]).astype(jnp.int32)


def pick(parts, own, target):
    peers = len(parts)
    result = parts[0]
    for step in range(1, peers):
        result = jnp.where((target - own + peers) % peers == step, parts[step], result)
    return result


def ahead(wide, peers, step):
    return [(w, w // peers * peers + (w % peers + step) % peers) for w in range(wide)]


def per_device(
    tokens,
    segment_ids,
    cotangent,
    w_qkv,
    b_qv,
    w_out,
    b_out,
    ls_attn,
    ln1_gain,
    ln1_bias,
    ln2_gain,
    ln2_bias,
    w_fc1,
    b_fc1,
    w_fc2,
    b_fc2,
    ls_mlp,
):
    geo = Geometry(lax.axis_size("wide"), tokens.shape[3])
    wide, peers, chunk, rows, cols = geo.wide, geo.peers, geo.chunk, geo.rows, geo.cols
    own = lax.axis_index("wide") % peers

    def regroup(array):
        return lax.all_to_all(array, "wide", split_axis=0, concat_axis=0, tiled=True)

    token_rows = regroup(tokens.reshape(wide, chunk, D)).reshape(rows, D)
    cotangent, segment_ids, token_rows = lax.optimization_barrier(
        (cotangent, segment_ids, token_rows)
    )
    ids_out = jnp.broadcast_to(segment_ids.reshape(GROUPS, 1, geo.piece), (GROUPS, peers, geo.piece))
    block_ids = regroup(ids_out.reshape(wide, geo.piece)).reshape(geo.slots)
    cotangent_rows = regroup(cotangent.reshape(wide, chunk, D)).reshape(rows, D)

    my_ids = lax.dynamic_index_in_dim(
        block_ids.reshape(wide, peers, chunk), own, 1, keepdims=False
    ).reshape(rows, 1)
    valid_rows = (my_ids >= 0).astype(F32)
    key_marks, query_marks = marks_of(block_ids, geo)
    table = tile_table(block_ids, own, geo)

    bias_all = jnp.concatenate([b_qv[:D], jnp.zeros((D,), F32), b_qv[D:]])
    w_heads = w_qkv.reshape(D, 3, peers, geo.real_cols)
    b_heads = bias_all.reshape(3, peers, geo.real_cols)
    o_heads = w_out.reshape(peers, geo.real_cols, D)
    spare = cols - geo.real_cols

    w_own = lax.dynamic_index_in_dim(w_heads, own, 2, keepdims=False)
    w_own = jnp.pad(w_own, ((0, 0), (0, 0), (0, spare))).reshape(D, 3 * cols)
    b_own = lax.dynamic_index_in_dim(b_heads, own, 1, keepdims=False)
    b_own = jnp.pad(b_own, ((0, 0), (0, spare))).reshape(3 * cols)

    def outward_of(step):
        o = lax.dynamic_index_in_dim(o_heads, (own + step) % peers, 0, keepdims=False)
        return jnp.pad(o, ((0, spare), (0, 0)))

    o_parts = [outward_of(step) for step in range(peers)]
    begins = [0]
    counts = [end - begin for begin, end in zip(begins, [*begins[1:], geo.pairs])]
    w_split = w_own.reshape(D, 3, geo.pairs, LANES)
    w_calls = [
        w_split[:, :, begin : begin + count].reshape(D, -1)
        for begin, count in zip(begins, counts)
    ]
    token_rows, w_own, w_calls, o_parts = lax.optimization_barrier(
        (token_rows, w_own, w_calls, o_parts)
    )

    def send(array, step):
        return lax.ppermute(array, "wide", ahead(wide, peers, step % peers))

    def peer_share(left, right):
        width = right.shape[1] // peers

        def product(step):
            start = (own + step) % peers * width
            some = lax.dynamic_slice_in_dim(right, start, width, 1)
            return lax.dot_general(left, some, (((0,), (0,)), ((), ())), preferred_element_type=F32)

        travels = [send(product(step).astype(BF16), step) for step in range(1, peers)]
        return (product(0) + sum(t.astype(F32) for t in travels)).astype(BF16)

    def scattered(array):
        return lax.psum_scatter(array, "narrow", scatter_dimension=0, tiled=True)

    def over_chips(array):
        return lax.psum(array, "wide", axis_index_groups=[
            list(range(p, wide, peers)) for p in range(peers)
        ])

    def held(*values):
        return lax.optimization_barrier(values)

    def over_peers(array):
        return lax.all_gather(array, "wide", axis_index_groups=[
            list(range(g, g + peers)) for g in range(0, wide, peers)
        ])

    inputs = token_rows.astype(F32)
    normed, norm_first_back = jax.vjp(layer_norm, inputs, ln1_gain, ln1_bias)
    normed_low = normed.astype(BF16)
    normed_parts = [normed_low] + [send(normed_low, step) for step in range(1, peers)]
    qkv_parts = [
        (dot_nn(part, w_own) + b_own).astype(BF16).reshape(wide, chunk, 3 * cols)
        for part in normed_parts
    ]
    *mixed_parts, lse = attend(geo, table, qkv_parts, key_marks, query_marks)
    mixed_parts, cotangent_rows = lax.optimization_barrier((mixed_parts, cotangent_rows))
    mixed_home = [
        (send(part, -step) if step else part).reshape(rows, cols)
        for step, part in enumerate(mixed_parts)
    ]
    mixed_rows = jnp.concatenate(mixed_home, 1)
    w_out_rel = jnp.concatenate(o_parts, 0)
    projected = dot_nn(mixed_rows, w_out_rel) + b_out
    hidden = inputs + ls_attn * projected
    second, norm_second_back = jax.vjp(layer_norm, hidden, ln2_gain, ln2_bias)
    second_low = second.astype(BF16)
    pre_act = dot_nn(second_low, w_fc1) + b_fc1
    activation, gelu_back = jax.vjp(gelu_exact, pre_act)
    act_low = activation.astype(BF16)
    mlp_out = dot_nn(act_low, w_fc2) + b_fc2
    result = ((hidden + ls_mlp * mlp_out) * valid_rows).astype(BF16)
    output = regroup(result.reshape(wide, chunk, D))
    grad_out = cotangent_rows.astype(F32) * valid_rows
    grad_ls_mlp = jnp.sum(grad_out * mlp_out, 0)
    grad_mlp = (ls_mlp * grad_out).astype(BF16)
    grad_b_fc2 = jnp.sum(grad_mlp.astype(F32), 0)
    grad_w_fc2 = peer_share(act_low, grad_mlp)
    grad_act = jnp.dot(grad_mlp, w_fc2.T, preferred_element_type=F32)
    grad_pre = gelu_back(grad_act)[0].astype(BF16)
    grad_b_fc1 = jnp.sum(grad_pre.astype(F32), 0)
    grad_w_fc1 = peer_share(second_low, grad_pre)
    grad_second = jnp.dot(grad_pre, w_fc1.T, preferred_element_type=F32)
    grad_hidden_norm, grad_ln2_gain, grad_ln2_bias = norm_second_back(grad_second)
    grad_hidden = grad_out + grad_hidden_norm
    grad_ls_attn = jnp.sum(grad_hidden * projected, 0)
    grad_proj = (ls_attn * grad_hidden).astype(BF16)
    grad_b_out = jnp.sum(grad_proj.astype(F32), 0)
    proj_parts = [grad_proj] + [send(grad_proj, step) for step in range(1, peers)]
    mixed_plain = jnp.concatenate(
        [pick([m[:, : geo.real_cols] for m in mixed_home], own, g) for g in range(peers)], 1
    )
    grad_w_out = peer_share(mixed_plain, grad_proj)
    grad_parts = [
        jnp.dot(part, o_parts[0].T, preferred_element_type=F32)
        .astype(BF16)
        .reshape(wide, chunk, cols)
        for part in proj_parts
    ]
    narrow = lax.axis_size("narrow")

    share, step_width = D // narrow, D // peers
    columns = grad_w_fc1.reshape(narrow, share, GROUPS * step_width)
    columns = [columns[:, :, k * step_width : (k + 1) * step_width] for k in range(GROUPS)]
    quarters = jnp.concatenate(
        [
            grad_w_fc2.reshape(narrow, GROUPS, share, step_width),
            jnp.stack(columns, 1),
            grad_w_out.reshape(narrow, GROUPS, share // GROUPS, step_width),
        ],
        2,
    ).reshape(-1, step_width)
    early = (grad_b_out, grad_ls_attn, grad_ln2_gain, grad_ln2_bias, grad_b_fc1, grad_b_fc2)
    grad_parts, quarters, early = lax.optimization_barrier((grad_parts, quarters, early))
    grad_b_out, grad_ls_attn, grad_ln2_gain, grad_ln2_bias, grad_b_fc1, grad_b_fc2 = early
    quarters = scattered(quarters).reshape(GROUPS, -1, step_width)

    def back(index):
        return attend_back(
            geo,
            begins[index],
            counts[index],
            table,
            qkv_parts,
            grad_parts,
            mixed_parts,
            lse,
            key_marks,
            query_marks,
        )

    calls = [back(0)]
    quarters, calls, output = held(quarters, calls, output)
    calls = [[part.reshape(rows, -1) for part in made] for made in calls]
    partial = [
        sum(
            jnp.dot(made[back], w.T, preferred_element_type=F32)
            for made, w in zip(calls, w_calls)
        )
        for back in range(peers)
    ]
    for step in range(1, peers):
        partial[step] = send(partial[step].astype(BF16), -step)
    grad_normed = partial[0]
    for step in range(1, peers):
        grad_normed = grad_normed + partial[step].astype(F32)
    sums = [
        sum(jnp.sum(part.astype(F32), 0) for part in made).reshape(3, 1, -1) for made in calls
    ]
    sums = jnp.concatenate(sums, 2)[:, :, : geo.real_cols]
    sums = jnp.where(jnp.arange(peers)[:, None] == own, sums, 0.0)
    grad_b_qv = sums[::2].reshape(2 * D)
    grad_inputs_norm, grad_ln1_gain, grad_ln1_bias = norm_first_back(grad_normed)
    grad_rows = (grad_hidden + grad_inputs_norm).astype(BF16)
    grad_rows, calls = held(grad_rows, calls)
    grad_tokens = regroup(grad_rows.reshape(wide, chunk, D))

    vectors = [
        grad_b_qv,
        grad_b_out,
        grad_ls_attn,
        grad_ln1_gain,
        grad_ln1_bias,
        grad_ln2_gain,
        grad_ln2_bias,
        grad_b_fc1,
        grad_b_fc2,
        grad_ls_mlp,
    ]
    flat = jnp.concatenate([v.reshape(narrow, -1) for v in vectors], 1)
    flat = jnp.pad(flat, ((0, 0), (0, -flat.shape[1] % (GROUPS * 8 * LANES))))
    flat = flat.reshape(narrow, GROUPS, -1, LANES)
    if narrow <= GROUPS:
        flat, *thirds, everything = reduce_everywhere(
            wide, peers, narrow, flat, normed_parts, calls, quarters
        )
    else:
        grad_w_qkv = []
        for made, count in zip(calls, counts):
            weight = sum(
                jnp.einsum("td,te->de", a, b, preferred_element_type=F32)
                for a, b in zip(normed_parts, made)
            ).astype(BF16)
            grad_w_qkv += [weight[:, k * 3 * LANES : (k + 1) * 3 * LANES] for k in range(count)]
        thirds = [w.reshape(narrow, GROUPS, -1, 3 * LANES) for w in grad_w_qkv]
        everything = over_peers(over_chips(quarters))
        flat, *thirds = (
            over_peers(over_chips(scattered(a))).reshape(peers, *a.shape[1:])
            for a in (flat, *thirds)
        )

    flat = sum(flat[p] for p in range(peers)).reshape(-1)
    small, start = [], 0
    for v in vectors:
        size = v.shape[0] // narrow
        small.append(flat[start : start + size])
        start += size
    blocks = []
    for third in range(3):
        for begin, count in zip(begins, counts):
            for pair in range(begin, begin + count):
                array, column = divmod(third * count + pair - begin, 3)
                width = min(LANES, geo.real_cols - pair * LANES)
                blocks.append((begin + array, column * LANES, width, third))
    if narrow <= GROUPS:
        *matrices, output, grad_tokens = finish(
            blocks, peers, share, thirds, everything, output, grad_tokens
        )
    else:
        matrices = assembled(blocks, peers, share, thirds, everything)
    done_qkv, done_out, done_fc1, done_fc2 = matrices

    return (
        output.reshape(tokens.shape),
        grad_tokens.reshape(tokens.shape),
        done_qkv,
        small[0],
        done_out,
        small[1],
        small[2],
        small[3],
        small[4],
        small[5],
        small[6],
        done_fc1,
        small[7],
        done_fc2,
        small[8],
        small[9],
    )


def solution(mesh):
    rows = P("narrow", "wide", None, None, None)
    placed = (rows, P("narrow", "wide", None, None), rows) + (P(),) * 14
    matrix, vector = P("narrow", None), P("narrow")
    return jax.shard_map(
        per_device,
        mesh=mesh,
        in_specs=placed,
        out_specs=(
            rows,
            rows,
            matrix,
            vector,
            matrix,
            vector,
            vector,
            vector,
            vector,
            vector,
            vector,
            matrix,
            vector,
            matrix,
            vector,
            vector,
        ),
        check_vma=False,
    )
```
